32 devices in a mesh: omega: 8 (over y, x, core), row: 4 (over z).
Axes of the slice: x: 2, y: 2, z: 4, core: 2. Of those that a mesh axis runs over, the one named last changes fastest.
Arguments:
- frames: float32 [128, 256, 1024], P('omega', 'row'), may hold values from -6 to 6
- thresholds: int32 [256], P('row'), may hold values from 0 to 31
- spot_boxes: int32 [3, 1024], P(None, ('omega', 'row')), may hold values from -1 to 1023, as said below
Outputs:
- peak_weight: float32 [128, 256, 1024], P('omega', 'row')
- moments: float32 [4, 1024], P(None, ('omega', 'row'))
The draws below stay inside these ranges and needn't reach their ends.
Inputs may be any that keep to these rules, and one draw needn't show every extreme that they name: `spot_boxes`: slot block d of 32 slots (d = omega index * the number of row indices + row index) lists boxes that lie wholly inside the frames and rows of that device; its live boxes fill the leading slots, each block has 1 to 32 of them, and one block has 32; empty slots hold -1 in all three entries.
All inputs are finite; a program needn't handle non-finite values.
Results may differ from the reference program's by a relative error of at most 0.0003.
Values sent between devices are 32-bit elements; how exact they have to be, the bound alone decides.
No kernel may reach another device: no remote copies, remote signals or barrier semaphores. Data moves between devices by JAX's collectives and lax.ppermute only.
A program may use at most 64 MiB of HBM per device.

```python
import jax
import jax.numpy as jnp
from jax import lax

FR_DEV = 16
ROWS_DEV = 64
COLS = 1024
CAP = 32
BW = 4
BOX_F = 8
BOX_R = 16
BOX_C = 16
FRAMES = 128
ROWS = 256
N_OMEGA = 8
N_ROW = 4


def draw_spot_boxes(key, part):
    blocks = N_OMEGA * N_ROW
    key_busy = jax.random.fold_in(key, 11)
    key_live = jax.random.fold_in(key, 12)
    key_frame = jax.random.fold_in(key, 13)
    key_row = jax.random.fold_in(key, 14)
    key_column = jax.random.fold_in(key, 15)
    block_ids = jnp.arange(blocks)
    omega_ids = block_ids // N_ROW
    row_ids = block_ids % N_ROW
    busiest = jax.random.randint(key_busy, (), 0, blocks)
    live = jax.random.randint(key_live, (blocks,), 1, CAP // 2 + 1)
    live = jnp.where(block_ids == busiest, CAP, live)
    first = jax.random.randint(key_frame, (blocks, CAP), 0, FR_DEV - BOX_F + 1) + omega_ids[:, None] * FR_DEV
    second = jax.random.randint(key_row, (blocks, CAP), 0, ROWS_DEV - BOX_R + 1) + row_ids[:, None] * ROWS_DEV
    third = jax.random.randint(key_column, (blocks, CAP), 0, COLS - BOX_C + 1)
    alive = jnp.arange(CAP)[None, :] < live[:, None]
    stacked = jnp.stack([first, second, third])
    stacked = jnp.where(alive[None], stacked, -1)
    return stacked.reshape(3, blocks * CAP).astype(jnp.int32)


def plant(result, rng, least, high):
    place = [jax.random.randint(jax.random.fold_in(rng, axis), (), 0, length) for axis, length in enumerate(result.shape)]
    longest = result.shape.index(max(result.shape))
    neighbour = place[:longest] + [(place[longest] + 1) % result.shape[longest]] + place[longest + 1:]
    return result.at[tuple(place)].set(least).at[tuple(neighbour)].set(high)


def level_of(key, shape, pieces, least, largest):
    factor_of, own = 1.0, jax.random.fold_in(key, 6)
    for dim, blocks in pieces:
        draws = jnp.exp(jax.random.uniform(jax.random.fold_in(own, dim), (blocks,), jnp.float32, least / len(pieces), largest / len(pieces)))
        factor_of = factor_of * jnp.repeat(draws, shape[dim] // blocks).reshape([-1 if axis == dim else 1 for axis in range(len(shape))])
    return factor_of


def noise(rng, extent, width, bound, pieces=(), held_as=jnp.bfloat16):
    values = width * jax.random.normal(rng, extent, jnp.float32)
    if pieces:
        values = values * level_of(rng, extent, pieces, -0.22, 0.18)
    return jnp.clip(values, -bound, bound).astype(held_as)


def setup_inputs(seed: int = 0) -> dict:
    key_of = jax.random.split(jax.random.key(seed), 4)
    frames = noise(key_of[0], (FRAMES, ROWS, COLS), 1.0, 6.0, ((0, 8), (1, 4)), jnp.float32)
    thresholds = plant(jax.random.randint(key_of[1], (ROWS,), 0, 32), jax.random.fold_in(key_of[1], 1), 0, 31).astype(jnp.int32)
    spot_boxes = draw_spot_boxes(jax.random.fold_in(key_of[3], 71), 0)
    return {"frames": frames, "thresholds": thresholds, "spot_boxes": spot_boxes}


SHARP = 8.0


def offsets_table(length):
    steps = jnp.arange(length).astype(jnp.float32)
    half = (length - 1) / 2.0
    return (steps - half) / half


def box_stats(weight, column):
    live = column[0] >= 0
    first = jnp.maximum(column[0], 0).astype(jnp.int32)
    second = jnp.maximum(column[1], 0).astype(jnp.int32)
    third = jnp.maximum(column[2], 0).astype(jnp.int32)
    patch = lax.dynamic_slice(weight, (first, second, third), (BOX_F, BOX_R, BOX_C))
    frame_off = offsets_table(BOX_F)[:, None, None]
    row_off = offsets_table(BOX_R)[None, :, None]
    column_off = offsets_table(BOX_C)[None, None, :]
    stats = jnp.stack([jnp.mean(patch), jnp.mean(patch * frame_off), jnp.mean(patch * row_off), jnp.mean(patch * column_off)])
    return jnp.where(live, stats, jnp.zeros_like(stats))


def one_frame(frames, level, index):
    reach = BW + 2
    span = 2 * BW + 1
    picks = ((jnp.arange(2 * reach + 1).astype(jnp.int32) - reach + index) % FRAMES).astype(jnp.int32)
    window = jnp.take(frames, picks, axis=0)
    total = window[0:5]
    for offset in range(1, span):
        total = total + window[offset:offset + 5]
    corrected = window[BW:BW + 5] - total / span
    smooth = (corrected[:-2] + 2.0 * corrected[1:-1] + corrected[2:]) * 0.25
    padded = jnp.pad(smooth, ((0, 0), (1, 1), (0, 0)))
    smooth = (padded[:, :-2] + 2.0 * padded[:, 1:-1] + padded[:, 2:]) * 0.25
    padded = jnp.pad(smooth, ((0, 0), (0, 0), (1, 1)))
    smooth = (padded[:, :, :-2] + 2.0 * padded[:, :, 1:-1] + padded[:, :, 2:]) * 0.25
    highest = jnp.maximum(jnp.maximum(smooth[0], smooth[1]), smooth[2])
    padded = jnp.pad(highest, ((1, 1), (0, 0)), mode="edge")
    highest = jnp.maximum(jnp.maximum(padded[:-2], padded[1:-1]), padded[2:])
    padded = jnp.pad(highest, ((0, 0), (1, 1)), mode="edge")
    highest = jnp.maximum(jnp.maximum(padded[:, :-2], padded[:, 1:-1]), padded[:, 2:])
    centre = smooth[1]
    return jnp.exp(SHARP * (centre - highest)) * jnp.maximum(centre - level[:, None], 0.0)


def reference(frames, thresholds, spot_boxes):
    level = thresholds.astype(jnp.float32) / 64.0
    weight = lax.map(lambda index: one_frame(frames, level, index), jnp.arange(FRAMES).astype(jnp.int32))
    stats = lax.map(lambda column: box_stats(weight, column), spot_boxes.T)
    return weight, stats.T
```

```python
import functools

import jax
import jax.numpy as jnp
from jax import lax
from jax.experimental import pallas as pl
from jax.experimental.pallas import tpu as pltpu
from jax.sharding import PartitionSpec as P

BW = 4
BOX_F = 8
BOX_R = 16
BOX_C = 16
SHARP = 8.0

SUB = 8
LANES = 128
REACH = BW + 2
SPAN = 2 * BW + 1
NEG = -1e30
SCALE = 1.0 / (SPAN * 64.0)


def next_row(tiles, sub):
    rolled = [pltpu.roll(v, SUB - 1, 0) for v in tiles]
    n = len(tiles)
    return [jnp.where(sub == SUB - 1, rolled[(t + 1) % n], rolled[t]) for t in range(n)]


def previous_row(tiles, sub):
    rolled = [pltpu.roll(v, 1, 0) for v in tiles]
    return [jnp.where(sub == 0, rolled[t - 1], rolled[t]) for t in range(len(tiles))]


def row_sums(tiles, sub):
    pairs = [a + b for a, b in zip(tiles, next_row(tiles, sub))]
    return [a + b for a, b in zip(pairs, previous_row(pairs, sub))]


def row_tops(tiles, sub):
    pairs = [jnp.maximum(a, b) for a, b in zip(tiles, next_row(tiles, sub))]
    return [jnp.maximum(a, b) for a, b in zip(pairs, previous_row(pairs, sub))]


def next_column(strips, lane, edge):
    rolled = [pltpu.roll(v, LANES - 1, 1) for v in strips] + [edge]
    return [jnp.where(lane == LANES - 1, rolled[j + 1], rolled[j]) for j in range(len(strips))]


def previous_column(strips, lane, edge):
    rolled = [edge] + [pltpu.roll(v, 1, 1) for v in strips]
    return [jnp.where(lane == 0, rolled[j], rolled[j + 1]) for j in range(len(strips))]


def column_stage(strips, lane):
    zero = jnp.zeros_like(strips[0])
    pairs = [a + b for a, b in zip(strips, next_column(strips, lane, zero))]
    sums = [(a + b) * SCALE for a, b in zip(pairs, previous_column(pairs, lane, strips[0]))]
    tops = [jnp.maximum(a, b) for a, b in zip(sums, next_column(sums, lane, sums[-1]))]
    tops = [jnp.maximum(a, b) for a, b in zip(tops, previous_column(tops, lane, tops[0]))]
    return sums, tops


def iotas():
    sub = lax.broadcasted_iota(jnp.int32, (SUB, LANES), 0)
    lane = lax.broadcasted_iota(jnp.int32, (SUB, LANES), 1)
    return sub, lane


def rows_of(t):
    return pl.ds(t * SUB, SUB)


def smooth_and_column_tops(flags, sec, smooth, tops, frames, tiles, halo, columns):
    sub, lane = iotas()
    off = ((sub == SUB - 1) & (flags[1] == 1)) | ((sub == 0) & (flags[2] == 1))

    def body(i, carry):
        for k in range(tiles):
            strips = [sec[i, rows_of(k), pl.ds(j * LANES, LANES)] for j in range(columns // LANES)]
            sums, highs = column_stage(strips, lane)
            for j in range(columns // LANES):
                at = pl.ds(j * LANES, LANES)
                if k == halo:
                    tops[i, rows_of(k), at] = jnp.where(off, NEG, highs[j])
                else:
                    smooth[i, rows_of(k), at] = sums[j]
                    tops[i, rows_of(k), at] = highs[j]
        return carry

    lax.fori_loop(0, frames, body, 0)


def weigh(smooth, tops, level, weight, place, count, tiles, outs, columns):
    sub, _ = iotas()

    def body(j, carry):
        at = pl.ds(pl.multiple_of(j * LANES, LANES), LANES)
        load = lambda i: [tops[i, rows_of(k), at] for k in range(tiles)]
        here = load(1)
        before = [jnp.maximum(a, b) for a, b in zip(load(0), here)]
        for i in range(1, count + 1):
            after = load(i + 1)
            pairs = [jnp.maximum(a, b) for a, b in zip(here, after)]
            highs = row_tops([jnp.maximum(a, b) for a, b in zip(before, pairs)], sub)
            here, before = after, pairs
            for k, o, v in outs:
                s = smooth[i, rows_of(k), at]
                w = jnp.exp(SHARP * (s - highs[k])) * jnp.maximum(s - level[rows_of(v), :], 0.0)
                weight[place(i), rows_of(o), at] = w
        return carry

    lax.fori_loop(0, columns // LANES, body, 0)


def box_sums(weight, sel, boxes, frame_of, count, row_of, rows, start):
    slots2 = sel.shape[1]
    f0, r0 = boxes[0:1, :], boxes[1:2, :]
    row = row_of(lax.broadcasted_iota(jnp.int32, (rows, slots2), 0)) - r0
    row_pick = jnp.where((row >= 0) & (row < BOX_R), 1.0, 0.0)
    row_odd = row_pick * (2 * row - (BOX_R - 1)).astype(jnp.float32)

    def body(i, carry):
        w = weight[i]
        high = w.astype(jnp.bfloat16)
        low = (w - high.astype(jnp.float32)).astype(jnp.bfloat16)
        table = sel[...]
        folded = jnp.dot(high, table, preferred_element_type=jnp.float32)
        folded = folded + jnp.dot(low, table, preferred_element_type=jnp.float32)
        frame = frame_of(i) - f0
        pick = jnp.where((frame >= 0) & (frame < BOX_F), 1.0, 0.0)
        odd = pick * (2 * frame - (BOX_F - 1)).astype(jnp.float32)
        plain = jnp.sum(folded * row_pick, axis=0, keepdims=True)
        by_row = jnp.sum(folded * row_odd, axis=0, keepdims=True)
        return (carry[0] + plain * pick, carry[1] + plain * odd, carry[2] + by_row * pick)

    return lax.fori_loop(0, count, body, start)


def early_kernel(
    flags, x, a, h, level, sel, boxes, out, own, sums, sec, smooth, tops, weight, sem, *, early, halo_first
):
    count, rows, columns = x.shape
    tiles = rows // SUB
    sub, _ = iotas()
    even = flags[0] == 1

    def body(j, carry):
        at = pl.ds(pl.multiple_of(j * LANES, LANES), LANES)

        def load(p):
            if p >= count:
                return None
            if p < 0:
                index = jnp.where(even, -1 - p, REACH + p)
                return [a[index, rows_of(t), at] for t in range(tiles)] + [h[index, :, at]]
            index = jnp.where(even, count - 1 - p, p)
            return [x[index, rows_of(t), at] for t in range(tiles)] + [h[halo_first + index, :, at]]

        window = load(-REACH)
        for p in range(1 - REACH, SPAN - REACH):
            window = [u + v for u, v in zip(window, load(p))]
        last_c = last_d = None
        for p in range(-2, count + 2):
            if p > -2:
                if p + BW < count:
                    window = [u + v for u, v in zip(window, load(p + BW))]
                window = [u - v for u, v in zip(window, load(p - BW - 1))]
            f = load(p)
            c = [-v for v in window] if f is None else [float(SPAN) * u - v for u, v in zip(f, window)]
            if last_c is not None:
                d = [u + v for u, v in zip(last_c, c)]
                if last_d is not None:
                    second = row_sums([u + v for u, v in zip(last_d, d)], sub)
                    q = p - 1
                    for t in range(tiles + 1):
                        if q <= early:
                            sec[q + 1, rows_of(t), at] = second[t]
                        if q >= early - 1:
                            own[q - early + 1, rows_of(t), at] = second[t]
                last_d = d
            last_c = c
        return carry

    lax.fori_loop(0, columns // LANES, body, 0)
    smooth_and_column_tops(flags, sec, smooth, tops, early + 2, tiles + 1, tiles, columns)
    weigh(
        smooth,
        tops,
        level,
        weight,
        lambda i: jnp.where(even, early - i, i - 1),
        early,
        tiles + 1,
        [(t, t, t) for t in range(tiles)],
        columns,
    )
    first = jnp.where(even, count - early, 0)
    copy = pltpu.make_async_copy(weight, out.at[pl.ds(first, early)], sem)
    copy.start()
    zero = jnp.zeros((1, sel.shape[1]), jnp.float32)
    result = box_sums(weight, sel, boxes, lambda i: first + i, early, lambda r: r, rows, (zero,) * 3)
    for i in range(3):
        sums[i : i + 1, :] = result[i]
    copy.wait()


def late_kernel(
    flags, own, b0, b1, h, level, sel, boxes, sums, _, out, stats, sec, smooth, tops, weight, sem, *, count, early
):
    late = count - early
    rows, columns = out.shape[1], out.shape[2]
    tiles = rows // SUB
    sub, _ = iotas()
    even = flags[0] == 1

    def body(j, carry):
        at = pl.ds(pl.multiple_of(j * LANES, LANES), LANES)

        def load(q):
            index = jnp.where(even, REACH - 1 - q, q)
            return (
                [b0[index, rows_of(0), at]]
                + [b1[index, rows_of(t), at] for t in range(tiles - 2)]
                + [b0[index, rows_of(1), at], h[index, :, at]]
            )

        for t in range(tiles + 1):
            for i in range(2):
                sec[i, rows_of(t), at] = own[i, rows_of(t), at]
        total = None
        c = []
        fresh = []
        for q in range(REACH):
            fresh.append(load(q))
            total = fresh[0] if q == 0 else [u + v for u, v in zip(total, fresh[q])]
            c.append([-v for v in total] if q < BW else [float(SPAN) * u - v for u, v in zip(fresh[q - BW], total)])
            d = c[0] if q == 0 else [u + v for u, v in zip(c[q - 1], c[q])]
            first = d if q == 0 else [u + v for u, v in zip(last_d, d)]
            last_d = d
            added = row_sums(first, sub)
            for t in range(tiles + 1):
                sec[q + 2, rows_of(t), at] = own[q + 2, rows_of(t), at] + added[t]
        return carry

    lax.fori_loop(0, columns // LANES, body, 0)
    smooth_and_column_tops(flags, sec, smooth, tops, late + 2, tiles + 1, tiles, columns)
    weigh(
        smooth,
        tops,
        level,
        weight,
        lambda i: jnp.where(even, late - i, i - 1),
        late,
        tiles + 1,
        [(t, t, t) for t in range(tiles)],
        columns,
    )
    first = jnp.where(even, 0, early)
    copy = pltpu.make_async_copy(weight, out.at[pl.ds(first, late)], sem)
    copy.start()
    start = tuple(sums[i : i + 1, :] for i in range(3))
    total, by_frame, by_row = box_sums(weight, sel, boxes, lambda i: first + i, late, lambda r: r, rows, start)
    slots = stats.shape[1]
    cells = float(BOX_F * BOX_R * BOX_C)
    stats[0:1, :] = total[:, :slots] / cells
    stats[1:2, :] = by_frame[:, :slots] / (cells * (BOX_F - 1))
    stats[2:3, :] = by_row[:, :slots] / (cells * (BOX_R - 1))
    stats[3:4, :] = total[:, slots:] / (cells * (BOX_C - 1))
    copy.wait()


def vmem():
    return pl.BlockSpec(memory_space=pltpu.VMEM)


def on_device(frames, thresholds, spot_boxes):
    count, rows, columns = frames.shape
    slots = spot_boxes.shape[1]
    early = count - REACH
    tiles = rows // SUB
    ring = lax.axis_size("omega")
    column = lax.axis_size("row")
    place = lax.axis_index("omega")
    even = place % 2 == 0
    partner = [(i, i ^ 1) for i in range(ring)]
    other = [(i, (i - 1) % ring if i % 2 == 0 else (i + 1) % ring) for i in range(ring)]
    up = [(i + 1, i) for i in range(column - 1)]
    down = [(i, i + 1) for i in range(column - 1)]

    far = lax.dynamic_slice_in_dim(frames, jnp.where(even, 0, count - REACH), REACH, axis=0)
    near = lax.dynamic_slice_in_dim(frames, jnp.where(even, count - REACH, 0), REACH, axis=0)
    edges = jnp.concatenate([far[:, :SUB], far[:, rows - SUB :]], axis=1)
    b0 = lax.ppermute(edges, "omega", other)
    b1 = lax.ppermute(far[:, SUB : rows - SUB], "omega", other)
    a = lax.ppermute(near, "omega", partner)

    lower = jnp.concatenate([a[:, rows - 2 :], frames[:, rows - 2 :], b0[:, 2 * SUB - 2 :]], axis=0)
    upper = jnp.concatenate([a[:, :2], frames[:, :2], b0[:, :2]], axis=0)
    above = lax.ppermute(lower, "row", down)
    below = lax.ppermute(upper, "row", up)
    h = jnp.concatenate([below, jnp.zeros((below.shape[0], SUB - 4, columns), jnp.float32), above], axis=1)

    row_place = lax.axis_index("row")
    flags = jnp.stack([even, row_place == 0, row_place == column - 1]).astype(jnp.int32)
    level = jnp.broadcast_to((thresholds.astype(jnp.float32) / 64.0)[:, None], (rows, LANES))
    live = spot_boxes[0] >= 0
    f0 = jnp.where(live, spot_boxes[0] - place * count, -BOX_F - count)
    r0 = spot_boxes[1] - row_place * rows
    boxes = jnp.stack([jnp.concatenate([f0, f0]), jnp.concatenate([r0, r0])])
    step = jnp.arange(columns)[:, None] - spot_boxes[2][None, :]
    inside = (step >= 0) & (step < BOX_C) & live[None, :]
    sel = jnp.where(
        jnp.concatenate([inside, inside], axis=1),
        jnp.concatenate([jnp.ones_like(step), 2 * step - (BOX_C - 1)], axis=1),
        0,
    ).astype(jnp.bfloat16)

    smem = pl.BlockSpec(memory_space=pltpu.SMEM)
    anywhere = pl.BlockSpec(memory_space=pl.ANY)
    padded = rows + SUB
    weight, own, sums = pl.pallas_call(
        functools.partial(early_kernel, early=early, halo_first=REACH),
        out_shape=(
            jax.ShapeDtypeStruct(frames.shape, jnp.float32),
            jax.ShapeDtypeStruct((REACH + 2, padded, columns), jnp.float32),
            jax.ShapeDtypeStruct((3, 2 * slots), jnp.float32),
        ),
        in_specs=[smem] + [vmem()] * 6,
        out_specs=(anywhere, vmem(), vmem()),
        scratch_shapes=[
            pltpu.VMEM((early + 2, padded, columns), jnp.float32),
            pltpu.VMEM((early + 2, padded, columns), jnp.float32),
            pltpu.VMEM((early + 2, padded, columns), jnp.float32),
            pltpu.VMEM((early, rows, columns), jnp.float32),
            pltpu.SemaphoreType.DMA,
        ],
        compiler_params=pltpu.CompilerParams(vmem_limit_bytes=56 << 20),
        cost_estimate=pl.CostEstimate(flops=40 * frames.size, bytes_accessed=16 << 20, transcendentals=0),
        name="early",
    )(flags, frames, a, h[: REACH + count], level, sel, boxes)
    weight, stats = pl.pallas_call(
        functools.partial(late_kernel, count=count, early=early),
        out_shape=(
            jax.ShapeDtypeStruct(frames.shape, jnp.float32),
            jax.ShapeDtypeStruct((4, slots), jnp.float32),
        ),
        in_specs=[smem] + [vmem()] * 8 + [anywhere],
        out_specs=(anywhere, vmem()),
        input_output_aliases={9: 0},
        scratch_shapes=[
            pltpu.VMEM((REACH + 2, padded, columns), jnp.float32),
            pltpu.VMEM((REACH + 2, padded, columns), jnp.float32),
            pltpu.VMEM((REACH + 2, padded, columns), jnp.float32),
            pltpu.VMEM((REACH, rows, columns), jnp.float32),
            pltpu.SemaphoreType.DMA,
        ],
        compiler_params=pltpu.CompilerParams(vmem_limit_bytes=56 << 20),
        cost_estimate=pl.CostEstimate(flops=20 * frames.size, bytes_accessed=8 << 20, transcendentals=0),
        name="late",
    )(flags, own, b0, b1, h[REACH + count :], level, sel, boxes, sums, weight)
    return weight, stats


def solution(mesh):
    return jax.shard_map(
        on_device,
        mesh=mesh,
        in_specs=(P("omega", "row", None), P("row"), P(None, ("omega", "row"))),
        out_specs=(P("omega", "row", None), P(None, ("omega", "row"))),
        check_vma=False,
    )
```

```python
import functools

import jax
import jax.numpy as jnp
from jax import lax
from jax.experimental import pallas as pl
from jax.experimental.pallas import tpu as pltpu
from jax.sharding import PartitionSpec as P

BW = 4
BOX_F = 8
BOX_R = 16
BOX_C = 16
SHARP = 8.0

SUB = 8
LANES = 128
REACH = BW + 2
SPAN = 2 * BW + 1
NEG = -1e30
TOP = 8
PIECES = ((0, 3), (3, 5), (5, 6))
SCALE = 1.0 / (SPAN * 64.0)


def frame_taps():
    three = {-1: 1, 0: 2, 1: 1}
    return [
        SPAN * three.get(d, 0) - sum(w for e, w in three.items() if abs(d - e) <= BW) for d in range(BW + 2)
    ]


def next_column(strips, lane, edge):
    rolled = [pltpu.roll(v, LANES - 1, 1) for v in strips] + [edge]
    return [jnp.where(lane == LANES - 1, rolled[j + 1], rolled[j]) for j in range(len(strips))]


def previous_column(strips, lane, edge):
    rolled = [edge] + [pltpu.roll(v, 1, 1) for v in strips]
    return [jnp.where(lane == 0, rolled[j], rolled[j + 1]) for j in range(len(strips))]


def iotas():
    sub = lax.broadcasted_iota(jnp.int32, (SUB, LANES), 0)
    lane = lax.broadcasted_iota(jnp.int32, (SUB, LANES), 1)
    return sub, lane


def rows_of(t):
    return pl.ds(t * SUB, SUB)


def store_rows(ref, i, j, tiles):
    for t, v in enumerate(tiles[:-1]):
        ref[i, j, pl.ds(TOP + t * SUB, SUB), :] = v
    ref[i, j, pl.ds(0, SUB), :] = tiles[-1]
    ref[i, j, pl.ds(TOP + (len(tiles) - 1) * SUB, SUB), :] = tiles[-1]


def smooth_stage(flags, first, smooth, count, shift, rows, strips):
    sub, lane = iotas()
    starts = [-1 + SUB * k for k in range(rows // SUB)] + [rows + 1 - SUB]
    above = (sub == 0) & (flags[1] == 1)
    below = (sub == SUB - 1) & (flags[2] == 1)
    zero = jnp.zeros((SUB, LANES), jnp.float32)

    def body(i, carry):
        for k, start in enumerate(starts):
            seconds = []
            for j in range(strips):
                a, b, c = (first[i, j, pl.ds(TOP + start + e, SUB), :] for e in (-1, 0, 1))
                seconds.append((a + b) + (b + c))
            pairs = [a + b for a, b in zip(seconds, next_column(seconds, lane, zero))]
            sums = [a + b for a, b in zip(pairs, previous_column(pairs, lane, seconds[0]))]
            for j in range(strips):
                v = sums[j]
                if k == 0:
                    v = jnp.where(above, NEG, v)
                if k == len(starts) - 1:
                    v = jnp.where(below, NEG, v)
                smooth[i + shift, j, pl.ds(TOP + start, SUB), :] = v
        return carry

    lax.fori_loop(0, count, body, 0)


def weigh(smooth_of, level, weight, place, count, rows, strips):
    _, lane = iotas()

    def body(t, carry):
        base = t * SUB + TOP
        at = pl.ds(pl.multiple_of(t * SUB, SUB), SUB)

        def row_tops(i):
            ref, index = smooth_of(i)
            loads = ([ref[index, j, pl.ds(base + e, SUB), :] for e in (-1, 0, 1)] for j in range(strips))
            return [jnp.maximum(jnp.maximum(a, b), c) for a, b, c in loads]

        here = row_tops(1)
        before = [jnp.maximum(a, b) for a, b in zip(row_tops(0), here)]
        floor = level[at, :]
        for i in range(1, count + 1):
            after = row_tops(i + 1)
            pairs = [jnp.maximum(a, b) for a, b in zip(here, after)]
            highs = [jnp.maximum(a, b) for a, b in zip(before, pairs)]
            here, before = after, pairs
            tops = [jnp.maximum(a, b) for a, b in zip(highs, next_column(highs, lane, highs[-1]))]
            tops = [jnp.maximum(a, b) for a, b in zip(tops, previous_column(tops, lane, tops[0]))]
            ref, index = smooth_of(i)
            for j in range(strips):
                s = ref[index, j, pl.ds(base, SUB), :]
                w = jnp.exp((SHARP * SCALE) * (s - tops[j])) * jnp.maximum(s * SCALE - floor, 0.0)
                weight[place(i), at, pl.ds(j * LANES, LANES)] = w
        return carry

    lax.fori_loop(0, rows // SUB, body, 0)


def box_sums(weight, sel, boxes, first, start):
    count, rows, columns = weight.shape
    group = 2 if count % 2 == 0 else 1
    slots2 = sel.shape[1]
    f0, r0 = boxes[0:1, :], boxes[1:2, :]
    row = lax.broadcasted_iota(jnp.int32, (rows, slots2), 0) - r0
    row_pick = jnp.where((row >= 0) & (row < BOX_R), 1.0, 0.0)
    row_odd = row_pick * (2 * row - (BOX_R - 1)).astype(jnp.float32)

    def body(i, carry):
        w = weight[pl.ds(i * group, group)].reshape(group * rows, columns)
        high = w.astype(jnp.bfloat16)
        low = (w - high.astype(jnp.float32)).astype(jnp.bfloat16)
        table = sel[...]
        folded = jnp.dot(high, table, preferred_element_type=jnp.float32)
        folded = folded + jnp.dot(low, table, preferred_element_type=jnp.float32)
        for k in range(group):
            part = folded[k * rows : (k + 1) * rows]
            frame = first + i * group + k - f0
            pick = jnp.where((frame >= 0) & (frame < BOX_F), 1.0, 0.0)
            odd = pick * (2 * frame - (BOX_F - 1)).astype(jnp.float32)
            plain = jnp.sum(part * row_pick, axis=0, keepdims=True)
            by_row = jnp.sum(part * row_odd, axis=0, keepdims=True)
            carry = (carry[0] + plain * pick, carry[1] + plain * odd, carry[2] + by_row * pick)
        return carry

    return lax.fori_loop(0, count // group, body, start)


def early_kernel(
    flags, x, a, h, level, sel, boxes, out, part, edge, sums, first, smooth, weight, sems, *, early
):
    count, rows, columns = x.shape
    tiles, strips = rows // SUB, columns // LANES
    even = flags[0] == 1

    def body(j, carry):
        at = pl.ds(pl.multiple_of(j * LANES, LANES), LANES)

        def load(p):
            if p >= count:
                return None
            if p < 0:
                index = jnp.where(even, -1 - p, REACH + p)
                where = count + index
                return [a[index, rows_of(t), at] for t in range(tiles)] + [h[where, :, at]]
            index = jnp.where(even, count - 1 - p, p)
            return [x[index, rows_of(t), at] for t in range(tiles)] + [h[index, :, at]]

        window = load(-REACH)
        for p in range(1 - REACH, SPAN - REACH):
            window = [u + v for u, v in zip(window, load(p))]
        last_c = last_d = None
        for p in range(-2, count + 2):
            if p > -2:
                if p + BW < count:
                    window = [u + v for u, v in zip(window, load(p + BW))]
                window = [u - v for u, v in zip(window, load(p - BW - 1))]
            f = load(p)
            c = [-v for v in window] if f is None else [float(SPAN) * u - v for u, v in zip(f, window)]
            if last_c is not None:
                d = [u + v for u, v in zip(last_c, c)]
                if last_d is not None:
                    result = [u + v for u, v in zip(last_d, d)]
                    q = p - 1
                    if q <= early:
                        store_rows(first, q + 1, j, result)
                    else:
                        for t, v in enumerate(result):
                            part[q - early - 1, j, rows_of(t), :] = v
                last_d = d
            last_c = c
        return carry

    lax.fori_loop(0, strips, body, 0)
    smooth_stage(flags, first, smooth, early + 2, 0, rows, strips)
    copy_edge = pltpu.make_async_copy(smooth.at[pl.ds(early, 2)], edge, sems.at[0])
    copy_edge.start()
    weigh(lambda i: (smooth, i), level, weight, lambda i: jnp.where(even, early - i, i - 1), early, rows, strips)
    start = jnp.where(even, count - early, 0)
    copy = pltpu.make_async_copy(weight, out.at[pl.ds(start, early)], sems.at[1])
    copy.start()
    zero = jnp.zeros((1, sel.shape[1]), jnp.float32)
    result = box_sums(weight, sel, boxes, start, (zero,) * 3)
    for i in range(3):
        sums[i : i + 1, :] = result[i]
    copy_edge.wait()
    copy.wait()


def late_kernel(flags, part, edge, b, b0, h, level, sel, boxes, sums, _, out, *rest, count, piece):
    begin, end = piece
    late = end - begin
    final = end == REACH
    if final:
        stats, first, smooth, weight, sems = rest
    else:
        new_part, new_edge, new_sums, first, smooth, weight, sems = rest
    rows, columns = out.shape[1], out.shape[2]
    tiles, strips = rows // SUB, columns // LANES
    even = flags[0] == 1
    taps = frame_taps()
    early = count - REACH

    def body(j, carry):
        at = pl.ds(pl.multiple_of(j * LANES, LANES), LANES)

        def load(q):
            index = jnp.where(even, end - 1 - q, q - begin)
            where = jnp.where(even, REACH - 1 - q, q)
            return (
                [b0[where, rows_of(0), at]]
                + [b[index, rows_of(t), at] for t in range(tiles - 2)]
                + [b0[where, rows_of(1), at], h[where, :, at]]
            )

        fresh = {q: load(q) for q in range(begin, end)}
        for i in range(REACH - begin):
            total = [part[i, j, rows_of(t), :] for t in range(tiles + 1)]
            for q in range(begin, end):
                distance = REACH - 1 + q - begin - i
                if abs(distance) < REACH:
                    tap = float(taps[abs(distance)])
                    if tap == -1.0:
                        total = [u - v for u, v in zip(total, fresh[q])]
                    else:
                        total = [u + tap * v for u, v in zip(total, fresh[q])]
            if i < late:
                store_rows(first, i, j, total)
            else:
                for t, v in enumerate(total):
                    new_part[i - late, j, rows_of(t), :] = v
        return carry

    lax.fori_loop(0, strips, body, 0)
    smooth_stage(flags, first, smooth, late, 0, rows, strips)
    copies = []
    if not final:
        copies.append(pltpu.make_async_copy(smooth.at[pl.ds(late - 2, 2)], new_edge, sems.at[0]))
        copies[0].start()
    weigh(
        lambda i: (edge, i) if i < 2 else (smooth, i - 2),
        level,
        weight,
        lambda i: jnp.where(even, late - i, i - 1),
        late,
        rows,
        strips,
    )
    place = jnp.where(even, REACH - end, early + begin)
    copies.append(pltpu.make_async_copy(weight, out.at[pl.ds(place, late)], sems.at[1]))
    copies[-1].start()
    start = tuple(sums[i : i + 1, :] for i in range(3))
    total, by_frame, by_row = box_sums(weight, sel, boxes, place, start)
    if final:
        slots = stats.shape[1]
        cells = float(BOX_F * BOX_R * BOX_C)
        stats[0:1, :] = total[:, :slots] / cells
        stats[1:2, :] = by_frame[:, :slots] / (cells * (BOX_F - 1))
        stats[2:3, :] = by_row[:, :slots] / (cells * (BOX_R - 1))
        stats[3:4, :] = total[:, slots:] / (cells * (BOX_C - 1))
    else:
        for i, v in enumerate((total, by_frame, by_row)):
            new_sums[i : i + 1, :] = v
    for copy in copies:
        copy.wait()


def shape(*sizes):
    return jax.ShapeDtypeStruct(sizes, jnp.float32)


def vmem():
    return pl.BlockSpec(memory_space=pltpu.VMEM)


def halo_rows(lower, upper):
    column = lax.axis_size("row")
    above = lax.ppermute(lower, "row", [(i, i + 1) for i in range(column - 1)])
    below = lax.ppermute(upper, "row", [(i + 1, i) for i in range(column - 1)])
    middle = jnp.zeros((below.shape[0], SUB - 4, below.shape[2]), jnp.float32)
    return jnp.concatenate([below, middle, above], axis=1)


def on_device(frames, thresholds, spot_boxes):
    count, rows, columns = frames.shape
    slots = spot_boxes.shape[1]
    early = count - REACH
    tiles, strips = rows // SUB, columns // LANES
    ring = lax.axis_size("omega")
    place = lax.axis_index("omega")
    even = place % 2 == 0
    partner = [(i, i ^ 1) for i in range(ring)]
    other = [(i, (i - 1) % ring if i % 2 == 0 else (i + 1) % ring) for i in range(ring)]

    tiled = frames.reshape(count, tiles, SUB, columns)
    far = lax.dynamic_slice_in_dim(tiled, jnp.where(even, 0, count - REACH), REACH, axis=0)
    b0 = lax.ppermute(far[:, :: tiles - 1], "omega", other).reshape(REACH, 2 * SUB, columns)
    near = lax.dynamic_slice_in_dim(frames, jnp.where(even, count - REACH, 0), REACH, axis=0)
    a = lax.ppermute(near, "omega", partner)
    pieces = []
    for begin, end in PIECES:
        piece = lax.dynamic_slice_in_dim(frames, jnp.where(even, begin, count - end), end - begin, axis=0)
        pieces.append(lax.ppermute(piece[:, SUB : rows - SUB], "omega", other))

    own_lower, own_upper = frames[:, rows - 2 :], frames[:, :2]
    a_lower, a_upper = a[:, rows - 2 :], a[:, :2]
    h1 = halo_rows(jnp.concatenate([own_lower, a_lower]), jnp.concatenate([own_upper, a_upper]))
    h2 = halo_rows(b0[:, 2 * SUB - 2 :], b0[:, :2])

    row_place = lax.axis_index("row")
    flags = jnp.stack([even, row_place == 0, row_place == lax.axis_size("row") - 1]).astype(jnp.int32)
    level = jnp.broadcast_to((thresholds.astype(jnp.float32) / 64.0)[:, None], (rows, LANES))
    live = spot_boxes[0] >= 0
    f0 = jnp.where(live, spot_boxes[0] - place * count, -BOX_F - count)
    r0 = spot_boxes[1] - row_place * rows
    boxes = jnp.stack([jnp.concatenate([f0, f0]), jnp.concatenate([r0, r0])])
    step = jnp.arange(columns)[:, None] - spot_boxes[2][None, :]
    inside = (step >= 0) & (step < BOX_C) & live[None, :]
    sel = jnp.where(
        jnp.concatenate([inside, inside], axis=1),
        jnp.concatenate([jnp.ones_like(step), 2 * step - (BOX_C - 1)], axis=1),
        0,
    ).astype(jnp.bfloat16)

    smem = pl.BlockSpec(memory_space=pltpu.SMEM)
    anywhere = pl.BlockSpec(memory_space=pl.ANY)
    padded = rows + 2 * TOP
    params = pltpu.CompilerParams(vmem_limit_bytes=56 << 20)
    weight, part, edge, sums = pl.pallas_call(
        functools.partial(early_kernel, early=early),
        out_shape=(
            shape(count, rows, columns),
            shape(REACH, strips, rows + SUB, LANES),
            shape(2, strips, padded, LANES),
            shape(3, 2 * slots),
        ),
        in_specs=[smem] + [vmem()] * 6,
        out_specs=(anywhere, vmem(), anywhere, vmem()),
        scratch_shapes=[
            pltpu.VMEM((early + 2, strips, padded, LANES), jnp.float32),
            pltpu.VMEM((early + 2, strips, padded, LANES), jnp.float32),
            pltpu.VMEM((early, rows, columns), jnp.float32),
            pltpu.SemaphoreType.DMA((2,)),
        ],
        compiler_params=params,
        cost_estimate=pl.CostEstimate(flops=40 * frames.size, bytes_accessed=16 << 20, transcendentals=0),
        name="early",
    )(flags, frames, a, h1, level, sel, boxes)
    for (begin, end), piece in zip(PIECES, pieces):
        final = end == REACH
        late = end - begin
        results = pl.pallas_call(
            functools.partial(late_kernel, count=count, piece=(begin, end)),
            out_shape=(shape(count, rows, columns),)
            + (
                (shape(4, slots),)
                if final
                else (
                    shape(REACH - end, strips, rows + SUB, LANES),
                    shape(2, strips, padded, LANES),
                    shape(3, 2 * slots),
                )
            ),
            in_specs=[smem] + [vmem()] * 9 + [anywhere],
            out_specs=(anywhere,) + ((vmem(),) if final else (vmem(), anywhere, vmem())),
            input_output_aliases={10: 0},
            scratch_shapes=[
                pltpu.VMEM((late, strips, padded, LANES), jnp.float32),
                pltpu.VMEM((late, strips, padded, LANES), jnp.float32),
                pltpu.VMEM((late, rows, columns), jnp.float32),
                pltpu.SemaphoreType.DMA((2,)),
            ],
            compiler_params=params,
            cost_estimate=pl.CostEstimate(flops=8 * late * rows * columns, bytes_accessed=4 << 20, transcendentals=0),
            name=f"late_{begin}",
        )(flags, part, edge, piece, b0, h2, level, sel, boxes, sums, weight)
        if final:
            weight, stats = results
        else:
            weight, part, edge, sums = results
    return weight, stats


def solution(mesh):
    return jax.shard_map(
        on_device,
        mesh=mesh,
        in_specs=(P("omega", "row", None), P("row"), P(None, ("omega", "row"))),
        out_specs=(P("omega", "row", None), P(None, ("omega", "row"))),
        check_vma=False,
    )
```

```python
import functools

import jax
import jax.numpy as jnp
from jax import lax
from jax.experimental import pallas as pl
from jax.experimental.pallas import tpu as pltpu
from jax.sharding import PartitionSpec as P


BW = 4
BOX_F = 8
BOX_R = 16
BOX_C = 16
SHARP = 8.0

SUB = 8
LANES = 128
REACH = BW + 2
SPAN = 2 * BW + 1
NEG = -1e30
ZPAD = 6
TOP = 8
PIECES = ((0, 5), (5, 6))
SCALE = 1.0 / (SPAN * 64.0)


def frame_taps():
    three = {-1: 1, 0: 2, 1: 1}
    return [
        SPAN * three.get(d, 0) - sum(w for e, w in three.items() if abs(d - e) <= BW) for d in range(BW + 2)
    ]


def next_column(strips, lane, edge):
    rolled = [pltpu.roll(v, LANES - 1, 1) for v in strips] + [edge]
    return [jnp.where(lane == LANES - 1, rolled[j + 1], rolled[j]) for j in range(len(strips))]


def previous_column(strips, lane, edge):
    rolled = [edge] + [pltpu.roll(v, 1, 1) for v in strips]
    return [jnp.where(lane == 0, rolled[j], rolled[j + 1]) for j in range(len(strips))]


def iotas():
    sub = lax.broadcasted_iota(jnp.int32, (SUB, LANES), 0)
    lane = lax.broadcasted_iota(jnp.int32, (SUB, LANES), 1)
    return sub, lane


def is_even():
    return lax.rem(lax.axis_index("omega"), 2) == 0


def row_is_even():
    return lax.rem(lax.axis_index("row"), 2) == 0


def rows_of(t):
    return pl.ds(t * SUB, SUB)


def store_rows(ref, i, j, tiles):
    for t, v in enumerate(tiles[:-1]):
        ref[i, j, pl.ds(TOP + t * SUB, SUB), :] = v
    ref[i, j, pl.ds(0, SUB), :] = tiles[-1]
    ref[i, j, pl.ds(TOP + (len(tiles) - 1) * SUB, SUB), :] = tiles[-1]


def smooth_stage(first, smooth, count, shift, rows, strips):
    sub, lane = iotas()
    starts = [-1 + SUB * k for k in range(rows // SUB)] + [rows + 1 - SUB]
    place = lax.axis_index("row")
    above = (sub == 0) & (place == 0)
    below = (sub == SUB - 1) & (place == lax.axis_size("row") - 1)
    zero = jnp.zeros((SUB, LANES), jnp.float32)

    def body(i, carry):
        for k, start in enumerate(starts):
            seconds = []
            for j in range(strips):
                a, b, c = (first[i, j, pl.ds(TOP + start + e, SUB), :] for e in (-1, 0, 1))
                seconds.append((a + b) + (b + c))
            pairs = [a + b for a, b in zip(seconds, next_column(seconds, lane, zero))]
            sums = [a + b for a, b in zip(pairs, previous_column(pairs, lane, seconds[0]))]
            for j in range(strips):
                v = sums[j]
                if k == 0:
                    v = jnp.where(above, NEG, v)
                if k == len(starts) - 1:
                    v = jnp.where(below, NEG, v)
                smooth[i + shift, j, pl.ds(TOP + start, SUB), :] = v
        return carry

    lax.fori_loop(0, count, body, 0)


def weigh(smooth_of, level, weight, place, count, rows, strips):
    _, lane = iotas()

    def body(t, carry):
        base = t * SUB + TOP
        at = pl.ds(pl.multiple_of(t * SUB, SUB), SUB)

        def row_tops(i):
            ref, index = smooth_of(i)
            loads = ([ref[index, j, pl.ds(base + e, SUB), :] for e in (-1, 0, 1)] for j in range(strips))
            return [jnp.maximum(jnp.maximum(a, b), c) for a, b, c in loads]

        here = row_tops(1)
        before = [jnp.maximum(a, b) for a, b in zip(row_tops(0), here)]
        floor = level[at, :]
        for i in range(1, count + 1):
            after = row_tops(i + 1)
            pairs = [jnp.maximum(a, b) for a, b in zip(here, after)]
            highs = [jnp.maximum(a, b) for a, b in zip(before, pairs)]
            here, before = after, pairs
            tops = [jnp.maximum(a, b) for a, b in zip(highs, next_column(highs, lane, highs[-1]))]
            tops = [jnp.maximum(a, b) for a, b in zip(tops, previous_column(tops, lane, tops[0]))]
            ref, index = smooth_of(i)
            for j in range(strips):
                s = ref[index, j, pl.ds(base, SUB), :]
                w = jnp.exp((SHARP * SCALE) * (s - tops[j])) * jnp.maximum(s * SCALE - floor, 0.0)
                weight[place(i), at, pl.ds(j * LANES, LANES)] = w
        return carry

    lax.fori_loop(0, rows // SUB, body, 0)


def box_sums(weight, sel, boxes, first, frames, start):
    count, rows, columns = weight.shape
    group = 2 if count % 2 == 0 else 1
    slots2 = sel.shape[1]
    frame_base = lax.axis_index("omega") * frames
    live = boxes[0:1, :] >= 0
    f0 = jnp.where(live, boxes[0:1, :] - frame_base, -BOX_F - frames)
    r0 = boxes[1:2, :] - lax.axis_index("row") * rows
    row = lax.broadcasted_iota(jnp.int32, (rows, slots2), 0) - r0
    row_pick = jnp.where((row >= 0) & (row < BOX_R), 1.0, 0.0)
    row_odd = row_pick * (2 * row - (BOX_R - 1)).astype(jnp.float32)

    def body(i, carry):
        w = weight[pl.ds(i * group, group)].reshape(group * rows, columns)
        high = w.astype(jnp.bfloat16)
        low = (w - high.astype(jnp.float32)).astype(jnp.bfloat16)
        table = sel[...]
        folded = jnp.dot(high, table, preferred_element_type=jnp.float32)
        folded = folded + jnp.dot(low, table, preferred_element_type=jnp.float32)
        for k in range(group):
            part = folded[k * rows : (k + 1) * rows]
            frame = first + i * group + k - f0
            pick = jnp.where((frame >= 0) & (frame < BOX_F), 1.0, 0.0)
            odd = pick * (2 * frame - (BOX_F - 1)).astype(jnp.float32)
            plain = jnp.sum(part * row_pick, axis=0, keepdims=True)
            by_row = jnp.sum(part * row_odd, axis=0, keepdims=True)
            carry = (carry[0] + plain * pick, carry[1] + plain * odd, carry[2] + by_row * pick)
        return carry

    return lax.fori_loop(0, count // group, body, start)


def halo_tile(z1, z2, index, j):
    sub, _ = iotas()
    even = row_is_even()
    shift1 = jnp.where(even, ZPAD, 0)
    head = (sub < SUB // 2) == even
    one = z1[j, pl.ds(2 * index + shift1, SUB), :]
    two = z2[j, pl.ds(2 * index + ZPAD - shift1, SUB), :]
    return jnp.where(head, one, two)


def edge_kernel(x, b0, sems):
    count, rows, _ = x.shape
    start = jnp.where(is_even(), 0, count - REACH)
    copies = [
        pltpu.make_async_copy(x.at[pl.ds(start, REACH), pl.ds(row, SUB)], b0.at[:, pl.ds(to, SUB)], sems.at[k])
        for k, (row, to) in enumerate(((0, 0), (rows - SUB, SUB)))
    ]
    for copy in copies:
        copy.start()
    for copy in copies:
        copy.wait()


def pack_kernel(x, near, *rest):
    count, rows, _ = x.shape
    *pieces, sems = rest
    even = is_even()
    copies = [pltpu.make_async_copy(x.at[pl.ds(jnp.where(even, count - REACH, 0), REACH)], near, sems.at[0])]
    for k, (begin, end) in enumerate(PIECES):
        start = jnp.where(even, begin, count - end)
        source = x.at[pl.ds(start, end - begin), pl.ds(SUB, rows - 2 * SUB)]
        copies.append(pltpu.make_async_copy(source, pieces[k], sems.at[k + 1]))
    for copy in copies:
        copy.start()
    for copy in copies:
        copy.wait()


def rows_kernel(*refs):
    *sources, z1, z2 = refs
    _, _ = iotas()
    even = row_is_even()
    strips = z1.shape[0]
    for j in range(strips):
        at = pl.ds(j * LANES, LANES)
        k = ZPAD
        for z in (z1, z2):
            z[j, 0:SUB, :] = jnp.zeros((SUB, LANES), jnp.float32)
            z[j, pl.ds(z.shape[1] - SUB, SUB), :] = jnp.zeros((SUB, LANES), jnp.float32)
        for source in sources:
            rows = source.shape[1]
            for i in range(source.shape[0]):
                upper, lower = source[i, 0:2, at], source[i, rows - 2 : rows, at]
                z1[j, k : k + 2, :] = jnp.where(even, lower, upper)
                z2[j, k : k + 2, :] = jnp.where(even, upper, lower)
                k += 2


def early_kernel(
    x, a, z1, z2, level, boxes, out, part, edge, sums, sel, first, smooth, weight, sems, *, early
):
    count, rows, columns = x.shape
    tiles, strips = rows // SUB, columns // LANES
    even = is_even()
    slots = boxes.shape[1] // 2
    step = lax.broadcasted_iota(jnp.int32, sel.shape, 0) - boxes[2:3, :]
    odd = lax.broadcasted_iota(jnp.int32, sel.shape, 1) >= slots
    value = jnp.where(odd, 2 * step - (BOX_C - 1), 1).astype(jnp.float32)
    inside = (step >= 0) & (step < BOX_C) & (boxes[0:1, :] >= 0)
    sel[...] = jnp.where(inside, value, 0.0).astype(jnp.bfloat16)

    def body(j, carry):
        at = pl.ds(pl.multiple_of(j * LANES, LANES), LANES)

        def load(p):
            if p >= count:
                return None
            if p < 0:
                index = jnp.where(even, -1 - p, REACH + p)
                return [a[index, rows_of(t), at] for t in range(tiles)] + [halo_tile(z1, z2, count + index, j)]
            index = jnp.where(even, count - 1 - p, p)
            return [x[index, rows_of(t), at] for t in range(tiles)] + [halo_tile(z1, z2, index, j)]

        window = load(-REACH)
        for p in range(1 - REACH, SPAN - REACH):
            window = [u + v for u, v in zip(window, load(p))]
        last_c = last_d = None
        for p in range(-2, count + 2):
            if p > -2:
                if p + BW < count:
                    window = [u + v for u, v in zip(window, load(p + BW))]
                window = [u - v for u, v in zip(window, load(p - BW - 1))]
            f = load(p)
            c = [-v for v in window] if f is None else [float(SPAN) * u - v for u, v in zip(f, window)]
            if last_c is not None:
                d = [u + v for u, v in zip(last_c, c)]
                if last_d is not None:
                    result = [u + v for u, v in zip(last_d, d)]
                    q = p - 1
                    if q <= early:
                        store_rows(first, q + 1, j, result)
                    else:
                        for t, v in enumerate(result):
                            part[q - early - 1, j, rows_of(t), :] = v
                last_d = d
            last_c = c
        return carry

    lax.fori_loop(0, strips, body, 0)
    smooth_stage(first, smooth, early + 2, 0, rows, strips)
    copy_edge = pltpu.make_async_copy(smooth.at[pl.ds(early, 2)], edge, sems.at[0])
    copy_edge.start()
    weigh(lambda i: (smooth, i), level, weight, lambda i: jnp.where(even, early - i, i - 1), early, rows, strips)
    start = jnp.where(even, count - early, 0)
    copy = pltpu.make_async_copy(weight, out.at[pl.ds(start, early)], sems.at[1])
    copy.start()
    zero = jnp.zeros((1, sel.shape[1]), jnp.float32)
    result = box_sums(weight, sel, boxes, start, count, (zero,) * 3)
    for i in range(3):
        sums[i : i + 1, :] = result[i]
    copy_edge.wait()
    copy.wait()


def late_kernel(part, edge, b, b0, z1, z2, level, sel, boxes, sums, _, out, *rest, count, piece):
    begin, end = piece
    late = end - begin
    final = end == REACH
    if final:
        stats, first, smooth, weight, sems = rest
    else:
        new_part, new_edge, new_sums, first, smooth, weight, sems = rest
    rows, columns = out.shape[1], out.shape[2]
    tiles, strips = rows // SUB, columns // LANES
    even = is_even()
    taps = frame_taps()
    early = count - REACH

    def body(j, carry):
        at = pl.ds(pl.multiple_of(j * LANES, LANES), LANES)

        def load(q):
            index = jnp.where(even, end - 1 - q, q - begin)
            where = jnp.where(even, REACH - 1 - q, q)
            return (
                [b0[where, rows_of(0), at]]
                + [b[index, rows_of(t), at] for t in range(tiles - 2)]
                + [b0[where, rows_of(1), at], halo_tile(z1, z2, where, j)]
            )

        fresh = {q: load(q) for q in range(begin, end)}
        for i in range(REACH - begin):
            total = [part[i, j, rows_of(t), :] for t in range(tiles + 1)]
            for q in range(begin, end):
                distance = REACH - 1 + q - begin - i
                if abs(distance) < REACH:
                    tap = float(taps[abs(distance)])
                    if tap == -1.0:
                        total = [u - v for u, v in zip(total, fresh[q])]
                    else:
                        total = [u + tap * v for u, v in zip(total, fresh[q])]
            if i < late:
                store_rows(first, i, j, total)
            else:
                for t, v in enumerate(total):
                    new_part[i - late, j, rows_of(t), :] = v
        return carry

    lax.fori_loop(0, strips, body, 0)
    smooth_stage(first, smooth, late, 0, rows, strips)
    copies = []
    if not final:
        copies.append(pltpu.make_async_copy(smooth.at[pl.ds(late - 2, 2)], new_edge, sems.at[0]))
        copies[0].start()
    weigh(
        lambda i: (edge, i) if i < 2 else (smooth, i - 2),
        level,
        weight,
        lambda i: jnp.where(even, late - i, i - 1),
        late,
        rows,
        strips,
    )
    place = jnp.where(even, REACH - end, early + begin)
    copies.append(pltpu.make_async_copy(weight, out.at[pl.ds(place, late)], sems.at[1]))
    copies[-1].start()
    start = tuple(sums[i : i + 1, :] for i in range(3))
    total, by_frame, by_row = box_sums(weight, sel, boxes, place, count, start)
    if final:
        slots = stats.shape[1]
        cells = float(BOX_F * BOX_R * BOX_C)
        stats[0:1, :] = total[:, :slots] / cells
        stats[1:2, :] = by_frame[:, :slots] / (cells * (BOX_F - 1))
        stats[2:3, :] = by_row[:, :slots] / (cells * (BOX_R - 1))
        stats[3:4, :] = total[:, slots:] / (cells * (BOX_C - 1))
    else:
        for i, v in enumerate((total, by_frame, by_row)):
            new_sums[i : i + 1, :] = v
    for copy in copies:
        copy.wait()


def shape(*sizes):
    return jax.ShapeDtypeStruct(sizes, jnp.float32)


def vmem():
    return pl.BlockSpec(memory_space=pltpu.VMEM)


def hbm():
    return pl.BlockSpec(memory_space=pltpu.HBM)


def row_exchange(sources, strips):
    column = lax.axis_size("row")
    frames = sum(v.shape[0] for v in sources)
    rows = shape(strips, 2 * frames + 2 * ZPAD, LANES)
    z1, z2 = pl.pallas_call(
        rows_kernel,
        out_shape=(rows, rows),
        in_specs=[vmem()] * len(sources),
        out_specs=(vmem(), vmem()),
        compiler_params=pltpu.CompilerParams(vmem_limit_bytes=1 << 20),
    )(*sources)
    pairs = [(i, i + 1) for i in range(0, column - 1, 2)]
    others = [(i, i + 1) for i in range(1, column - 1, 2)]
    both = lambda ps: ps + [(j, i) for i, j in ps]
    return lax.ppermute(z1, "row", both(pairs)), lax.ppermute(z2, "row", both(others))


def steps(frames, thresholds, spot_boxes):
    count, rows, columns = frames.shape
    slots = spot_boxes.shape[1]
    early = count - REACH
    strips = columns // LANES
    ring = lax.axis_size("omega")
    partner = [(i, i ^ 1) for i in range(ring)]
    other = [(i, (i - 1) % ring if i % 2 == 0 else (i + 1) % ring) for i in range(ring)]

    in_hbm = pltpu.with_memory_space_constraint(frames, pltpu.HBM)
    small = pltpu.CompilerParams(vmem_limit_bytes=1 << 20)
    edges = pl.pallas_call(
        edge_kernel,
        out_shape=shape(REACH, 2 * SUB, columns),
        in_specs=[hbm()],
        out_specs=vmem(),
        scratch_shapes=[pltpu.SemaphoreType.DMA((2,))],
        compiler_params=small,
        name="edge",
    )(in_hbm)
    b0 = lax.ppermute(edges, "omega", other)
    near, *pieces = pl.pallas_call(
        pack_kernel,
        out_shape=(shape(REACH, rows, columns),)
        + tuple(shape(end - begin, rows - 2 * SUB, columns) for begin, end in PIECES),
        in_specs=[hbm()],
        out_specs=(vmem(),) * (1 + len(PIECES)),
        scratch_shapes=[pltpu.SemaphoreType.DMA((1 + len(PIECES),))],
        compiler_params=small,
        name="pack",
    )(in_hbm)
    a = lax.ppermute(near, "omega", partner)
    pieces = [lax.ppermute(piece, "omega", other) for piece in pieces]
    z1, z2 = row_exchange([frames, a], strips)
    far1, far2 = row_exchange([b0], strips)

    level = jnp.broadcast_to((thresholds.astype(jnp.float32) / 64.0)[:, None], (rows, LANES))
    boxes = jnp.concatenate([spot_boxes, spot_boxes], axis=1)

    padded = rows + 2 * TOP
    weight, part, edge, sums, sel = pl.pallas_call(
        functools.partial(early_kernel, early=early),
        out_shape=(
            shape(count, rows, columns),
            shape(REACH, strips, rows + SUB, LANES),
            shape(2, strips, padded, LANES),
            shape(3, 2 * slots),
            jax.ShapeDtypeStruct((columns, 2 * slots), jnp.bfloat16),
        ),
        in_specs=[vmem()] * 6,
        out_specs=(hbm(), vmem(), vmem(), vmem(), vmem()),
        scratch_shapes=[
            pltpu.VMEM((early + 2, strips, padded, LANES), jnp.float32),
            pltpu.VMEM((early + 2, strips, padded, LANES), jnp.float32),
            pltpu.VMEM((early, rows, columns), jnp.float32),
            pltpu.SemaphoreType.DMA((2,)),
        ],
        compiler_params=pltpu.CompilerParams(vmem_limit_bytes=14 << 20),
        cost_estimate=pl.CostEstimate(flops=40 * frames.size, bytes_accessed=16 << 20, transcendentals=0),
        name="early",
    )(frames, a, z1, z2, level, boxes)
    for (begin, end), piece in zip(PIECES, pieces):
        final = end == REACH
        late = end - begin
        results = pl.pallas_call(
            functools.partial(late_kernel, count=count, piece=(begin, end)),
            out_shape=(shape(count, rows, columns),)
            + (
                (shape(4, slots),)
                if final
                else (
                    shape(REACH - end, strips, rows + SUB, LANES),
                    shape(2, strips, padded, LANES),
                    shape(3, 2 * slots),
                )
            ),
            in_specs=[vmem()] * 10 + [hbm()],
            out_specs=(hbm(),) + ((vmem(),) if final else (vmem(), vmem(), vmem())),
            input_output_aliases={10: 0},
            scratch_shapes=[
                pltpu.VMEM((late, strips, padded, LANES), jnp.float32),
                pltpu.VMEM((late, strips, padded, LANES), jnp.float32),
                pltpu.VMEM((late, rows, columns), jnp.float32),
                pltpu.SemaphoreType.DMA((2,)),
            ],
            compiler_params=pltpu.CompilerParams(vmem_limit_bytes=14 << 20),
            cost_estimate=pl.CostEstimate(flops=8 * late * rows * columns, bytes_accessed=4 << 20, transcendentals=0),
        )(part, edge, piece, b0, far1, far2, level, sel, boxes, sums, weight)
        if final:
            weight, stats = results
        else:
            weight, part, edge, sums = results
    return weight, stats


def solution(mesh):
    return jax.shard_map(
        steps,
        mesh=mesh,
        in_specs=(P("omega", "row", None), P("row"), P(None, ("omega", "row"))),
        out_specs=(P("omega", "row", None), P(None, ("omega", "row"))),
        check_vma=False,
    )
```

```python
import functools

import jax
import jax.numpy as jnp
from jax import lax
from jax.experimental import pallas as pl
from jax.experimental.pallas import tpu as pltpu
from jax.sharding import PartitionSpec as P


BW = 4
BOX_F = 8
BOX_R = 16
BOX_C = 16
SHARP = 8.0

SUB = 8
LANES = 128
REACH = BW + 2
SPAN = 2 * BW + 1
NEG = -1e30
ZPAD = 6
TOP = 8
PIECES = ((0, 4), (4, 5), (5, 6))
SCALE = 1.0 / (SPAN * 64.0)


def frame_taps():
    three = {-1: 1, 0: 2, 1: 1}
    return [
        SPAN * three.get(d, 0) - sum(w for e, w in three.items() if abs(d - e) <= BW) for d in range(BW + 2)
    ]


def next_column(strips, lane, edge):
    rolled = [pltpu.roll(v, LANES - 1, 1) for v in strips] + [edge]
    return [jnp.where(lane == LANES - 1, rolled[j + 1], rolled[j]) for j in range(len(strips))]


def previous_column(strips, lane, edge):
    rolled = [edge] + [pltpu.roll(v, 1, 1) for v in strips]
    return [jnp.where(lane == 0, rolled[j], rolled[j + 1]) for j in range(len(strips))]


def column_tops(strips, lane):
    tops = [jnp.maximum(a, b) for a, b in zip(strips, next_column(strips, lane, strips[-1]))]
    return [jnp.maximum(a, b) for a, b in zip(tops, previous_column(tops, lane, tops[0]))]


def iotas():
    sub = lax.broadcasted_iota(jnp.int32, (SUB, LANES), 0)
    lane = lax.broadcasted_iota(jnp.int32, (SUB, LANES), 1)
    return sub, lane


def is_even():
    return lax.rem(lax.axis_index("omega"), 2) == 0


def row_is_even():
    return lax.rem(lax.axis_index("row"), 2) == 0


def rows_of(t):
    return pl.ds(t * SUB, SUB)


def store_rows(ref, i, j, tiles):
    for t, v in enumerate(tiles[:-1]):
        ref[i, j, pl.ds(TOP + t * SUB, SUB), :] = v
    ref[i, j, pl.ds(0, SUB), :] = tiles[-1]
    ref[i, j, pl.ds(TOP + (len(tiles) - 1) * SUB, SUB), :] = tiles[-1]


def smooth_stage(first, smooth, count, shift, rows, strips):
    sub, lane = iotas()
    starts = [-1 + SUB * k for k in range(rows // SUB)] + [rows + 1 - SUB]
    place = lax.axis_index("row")
    above = (sub == 0) & (place == 0)
    below = (sub == SUB - 1) & (place == lax.axis_size("row") - 1)
    zero = jnp.zeros((SUB, LANES), jnp.float32)

    def body(i, carry):
        for k, start in enumerate(starts):
            seconds = []
            for j in range(strips):
                a, b, c = (first[i, j, pl.ds(TOP + start + e, SUB), :] for e in (-1, 0, 1))
                seconds.append((a + b) + (b + c))
            pairs = [a + b for a, b in zip(seconds, next_column(seconds, lane, zero))]
            sums = [a + b for a, b in zip(pairs, previous_column(pairs, lane, seconds[0]))]
            for j in range(strips):
                v = sums[j]
                if k == 0:
                    v = jnp.where(above, NEG, v)
                if k == len(starts) - 1:
                    v = jnp.where(below, NEG, v)
                smooth[i + shift, j, pl.ds(TOP + start, SUB), :] = v
        return carry

    lax.fori_loop(0, count, body, 0)


def row_tops(ref, i, base, strips):
    loads = ([ref[i, j, pl.ds(base + e, SUB), :] for e in (-1, 0, 1)] for j in range(strips))
    return [jnp.maximum(jnp.maximum(a, b), c) for a, b, c in loads]


def weight_of(s, top, floor):
    return jnp.exp((SHARP * SCALE) * (s - top)) * jnp.maximum(s * SCALE - floor, 0.0)


def weigh(smooth_of, level, weight, place, count, rows, strips, tail=None):
    _, lane = iotas()

    def body(t, carry):
        base = t * SUB + TOP
        at = pl.ds(pl.multiple_of(t * SUB, SUB), SUB)
        tops_of = lambda i: row_tops(*smooth_of(i), base, strips)
        here = tops_of(1)
        before = [jnp.maximum(a, b) for a, b in zip(tops_of(0), here)]
        floor = level[at, :]
        for i in range(1, count + 1):
            after = tops_of(i + 1)
            pairs = [jnp.maximum(a, b) for a, b in zip(here, after)]
            highs = [jnp.maximum(a, b) for a, b in zip(before, pairs)]
            here, before = after, pairs
            tops = column_tops(highs, lane)
            ref, index = smooth_of(i)
            for j in range(strips):
                s = ref[index, j, pl.ds(base, SUB), :]
                weight[place(i), at, pl.ds(j * LANES, LANES)] = weight_of(s, tops[j], floor)
        if tail is not None:
            for j, v in enumerate(column_tops(before, lane)):
                tail[j, at, :] = v
        return carry

    lax.fori_loop(0, rows // SUB, body, 0)


def weigh_last(smooth, centre, tail, level, weight, rows, strips):
    _, lane = iotas()
    for t in range(rows // SUB):
        base = t * SUB + TOP
        at = pl.ds(t * SUB, SUB)
        tops = column_tops(row_tops(smooth, 0, base, strips), lane)
        floor = level[at, :]
        for j in range(strips):
            s = centre[j, pl.ds(base, SUB), :]
            top = jnp.maximum(tops[j], tail[j, at, :])
            weight[0, at, pl.ds(j * LANES, LANES)] = weight_of(s, top, floor)


def box_sums(weight, sel, boxes, first, frames, start):
    count, rows, columns = weight.shape
    group = 2 if count % 2 == 0 else 1
    slots2 = sel.shape[1]
    frame_base = lax.axis_index("omega") * frames
    live = boxes[0:1, :] >= 0
    f0 = jnp.where(live, boxes[0:1, :] - frame_base, -BOX_F - frames)
    r0 = boxes[1:2, :] - lax.axis_index("row") * rows
    row = lax.broadcasted_iota(jnp.int32, (rows, slots2), 0) - r0
    row_pick = jnp.where((row >= 0) & (row < BOX_R), 1.0, 0.0)
    row_odd = row_pick * (2 * row - (BOX_R - 1)).astype(jnp.float32)

    def body(i, carry):
        w = weight[pl.ds(i * group, group)].reshape(group * rows, columns)
        high = w.astype(jnp.bfloat16)
        low = (w - high.astype(jnp.float32)).astype(jnp.bfloat16)
        table = sel[...]
        folded = jnp.dot(high, table, preferred_element_type=jnp.float32)
        folded = folded + jnp.dot(low, table, preferred_element_type=jnp.float32)
        for k in range(group):
            part = folded[k * rows : (k + 1) * rows]
            frame = first + i * group + k - f0
            pick = jnp.where((frame >= 0) & (frame < BOX_F), 1.0, 0.0)
            odd = pick * (2 * frame - (BOX_F - 1)).astype(jnp.float32)
            plain = jnp.sum(part * row_pick, axis=0, keepdims=True)
            by_row = jnp.sum(part * row_odd, axis=0, keepdims=True)
            carry = (carry[0] + plain * pick, carry[1] + plain * odd, carry[2] + by_row * pick)
        return carry

    return lax.fori_loop(0, count // group, body, start)


def halo_tile(z1, z2, index, j):
    sub, _ = iotas()
    even = row_is_even()
    shift1 = jnp.where(even, ZPAD, 0)
    head = (sub < SUB // 2) == even
    one = z1[j, pl.ds(2 * index + shift1, SUB), :]
    two = z2[j, pl.ds(2 * index + ZPAD - shift1, SUB), :]
    place = lax.axis_index("row")
    inside = (sub >= SUB // 2) | (place != lax.axis_size("row") - 1)
    inside = inside & ((sub < SUB // 2) | (place != 0))
    return jnp.where(inside, jnp.where(head, one, two), 0.0)


def edge_kernel(x, b0, sems):
    count, rows, _ = x.shape
    start = jnp.where(is_even(), 0, count - REACH)
    copies = [
        pltpu.make_async_copy(x.at[pl.ds(start, REACH), pl.ds(row, SUB)], b0.at[:, pl.ds(to, SUB)], sems.at[k])
        for k, (row, to) in enumerate(((0, 0), (rows - SUB, SUB)))
    ]
    for copy in copies:
        copy.start()
    for copy in copies:
        copy.wait()


def pack_kernel(x, near, *rest):
    count, rows, _ = x.shape
    *pieces, sems = rest
    even = is_even()
    copies = [pltpu.make_async_copy(x.at[pl.ds(jnp.where(even, count - REACH, 0), REACH)], near, sems.at[0])]
    for k, (begin, end) in enumerate(PIECES):
        start = jnp.where(even, begin, count - end)
        source = x.at[pl.ds(start, end - begin), pl.ds(SUB, rows - 2 * SUB)]
        copies.append(pltpu.make_async_copy(source, pieces[k], sems.at[k + 1]))
    for copy in copies:
        copy.start()
    for copy in copies:
        copy.wait()


def rows_kernel(*refs):
    *sources, z1, z2 = refs
    _, _ = iotas()
    even = row_is_even()
    strips = z1.shape[0]
    for j in range(strips):
        at = pl.ds(j * LANES, LANES)
        k = ZPAD
        for z in (z1, z2):
            z[j, 0:SUB, :] = jnp.zeros((SUB, LANES), jnp.float32)
            z[j, pl.ds(z.shape[1] - SUB, SUB), :] = jnp.zeros((SUB, LANES), jnp.float32)
        for source in sources:
            rows = source.shape[1]
            for i in range(source.shape[0]):
                upper, lower = source[i, 0:2, at], source[i, rows - 2 : rows, at]
                z1[j, k : k + 2, :] = jnp.where(even, lower, upper)
                z2[j, k : k + 2, :] = jnp.where(even, upper, lower)
                k += 2


def early_kernel(
    x, a, z1, z2, level, boxes, out, part, edge, sums, sel, first, smooth, weight, sems, *, early
):
    count, rows, columns = x.shape
    tiles, strips = rows // SUB, columns // LANES
    even = is_even()
    slots = boxes.shape[1] // 2
    step = lax.broadcasted_iota(jnp.int32, sel.shape, 0) - boxes[2:3, :]
    odd = lax.broadcasted_iota(jnp.int32, sel.shape, 1) >= slots
    value = jnp.where(odd, 2 * step - (BOX_C - 1), 1).astype(jnp.float32)
    inside = (step >= 0) & (step < BOX_C) & (boxes[0:1, :] >= 0)
    sel[...] = jnp.where(inside, value, 0.0).astype(jnp.bfloat16)

    def body(j, carry):
        at = pl.ds(pl.multiple_of(j * LANES, LANES), LANES)

        def load(p):
            if p >= count:
                return None
            if p < 0:
                index = jnp.where(even, -1 - p, REACH + p)
                return [a[index, rows_of(t), at] for t in range(tiles)] + [halo_tile(z1, z2, count + index, j)]
            index = jnp.where(even, count - 1 - p, p)
            return [x[index, rows_of(t), at] for t in range(tiles)] + [halo_tile(z1, z2, index, j)]

        window = load(-REACH)
        for p in range(1 - REACH, SPAN - REACH):
            window = [u + v for u, v in zip(window, load(p))]
        last_c = last_d = None
        for p in range(-2, count + 2):
            if p > -2:
                if p + BW < count:
                    window = [u + v for u, v in zip(window, load(p + BW))]
                window = [u - v for u, v in zip(window, load(p - BW - 1))]
            f = load(p)
            c = [-v for v in window] if f is None else [float(SPAN) * u - v for u, v in zip(f, window)]
            if last_c is not None:
                d = [u + v for u, v in zip(last_c, c)]
                if last_d is not None:
                    result = [u + v for u, v in zip(last_d, d)]
                    q = p - 1
                    if q <= early:
                        store_rows(first, q + 1, j, result)
                    else:
                        for t, v in enumerate(result):
                            part[q - early - 1, j, rows_of(t), :] = v
                last_d = d
            last_c = c
        return carry

    lax.fori_loop(0, strips, body, 0)
    smooth_stage(first, smooth, early + 2, 0, rows, strips)
    copy_edge = pltpu.make_async_copy(smooth.at[pl.ds(early, 2)], edge, sems.at[0])
    copy_edge.start()
    weigh(lambda i: (smooth, i), level, weight, lambda i: jnp.where(even, early - i, i - 1), early, rows, strips)
    start = jnp.where(even, count - early, 0)
    copy = pltpu.make_async_copy(weight, out.at[pl.ds(start, early)], sems.at[1])
    copy.start()
    zero = jnp.zeros((1, sel.shape[1]), jnp.float32)
    result = box_sums(weight, sel, boxes, start, count, (zero,) * 3)
    for i in range(3):
        sums[i : i + 1, :] = result[i]
    copy_edge.wait()
    copy.wait()


def late_kernel(part, b, b0, z1, z2, level, sel, boxes, sums, *rest, count, piece):
    begin, end = piece
    late = end - begin
    final = end == REACH
    ahead = end == REACH - 1
    if final:
        edge, tail, _, out, *rest = rest
    else:
        edge, _, out, *rest = rest
    if final:
        stats, first, smooth, weight, sems = rest
    elif ahead:
        new_part, new_edge, tail, new_sums, first, smooth, weight, sems = rest
    else:
        new_part, new_edge, new_sums, first, smooth, weight, sems = rest
    rows, columns = out.shape[1], out.shape[2]
    tiles, strips = rows // SUB, columns // LANES
    even = is_even()
    taps = frame_taps()
    early = count - REACH

    def body(j, carry):
        at = pl.ds(pl.multiple_of(j * LANES, LANES), LANES)

        def load(q):
            index = jnp.where(even, end - 1 - q, q - begin)
            where = jnp.where(even, REACH - 1 - q, q)
            return (
                [b0[where, rows_of(0), at]]
                + [b[index, rows_of(t), at] for t in range(tiles - 2)]
                + [b0[where, rows_of(1), at], halo_tile(z1, z2, where, j)]
            )

        fresh = {q: load(q) for q in range(begin, end)}
        for i in range(REACH - begin):
            total = [part[i, j, rows_of(t), :] for t in range(tiles + 1)]
            for q in range(begin, end):
                distance = REACH - 1 + q - begin - i
                if abs(distance) < REACH:
                    tap = float(taps[abs(distance)])
                    if tap == -1.0:
                        total = [u - v for u, v in zip(total, fresh[q])]
                    else:
                        total = [u + tap * v for u, v in zip(total, fresh[q])]
            if i < late:
                store_rows(first, i, j, total)
            else:
                for t, v in enumerate(total):
                    new_part[i - late, j, rows_of(t), :] = v
        return carry

    lax.fori_loop(0, strips, body, 0)
    smooth_stage(first, smooth, late, 0, rows, strips)
    copies = []
    if final:
        weigh_last(smooth, edge, tail, level, weight, rows, strips)
    else:
        if ahead:
            copies.append(pltpu.make_async_copy(smooth.at[late - 1], new_edge, sems.at[0]))
        else:
            copies.append(pltpu.make_async_copy(smooth.at[pl.ds(late - 2, 2)], new_edge, sems.at[0]))
        copies[0].start()
        weigh(
            lambda i: (edge, i) if i < 2 else (smooth, i - 2),
            level,
            weight,
            lambda i: jnp.where(even, late - i, i - 1),
            late,
            rows,
            strips,
            tail if ahead else None,
        )
    place = jnp.where(even, REACH - end, early + begin)
    copies.append(pltpu.make_async_copy(weight, out.at[pl.ds(place, late)], sems.at[1]))
    copies[-1].start()
    start = tuple(sums[i : i + 1, :] for i in range(3))
    total, by_frame, by_row = box_sums(weight, sel, boxes, place, count, start)
    if final:
        slots = stats.shape[1]
        cells = float(BOX_F * BOX_R * BOX_C)
        stats[0:1, :] = total[:, :slots] / cells
        stats[1:2, :] = by_frame[:, :slots] / (cells * (BOX_F - 1))
        stats[2:3, :] = by_row[:, :slots] / (cells * (BOX_R - 1))
        stats[3:4, :] = total[:, slots:] / (cells * (BOX_C - 1))
    else:
        for i, v in enumerate((total, by_frame, by_row)):
            new_sums[i : i + 1, :] = v
    for copy in copies:
        copy.wait()


def shape(*sizes):
    return jax.ShapeDtypeStruct(sizes, jnp.float32)


def vmem():
    return pl.BlockSpec(memory_space=pltpu.VMEM)


def hbm():
    return pl.BlockSpec(memory_space=pltpu.HBM)


def row_exchange(sources, strips):
    ring, column = lax.axis_size("omega"), lax.axis_size("row")
    frames = sum(v.shape[0] for v in sources)
    rows = shape(strips, 2 * frames + 2 * ZPAD, LANES)
    z1, z2 = pl.pallas_call(
        rows_kernel,
        out_shape=(rows, rows),
        in_specs=[vmem()] * len(sources),
        out_specs=(vmem(), vmem()),
        compiler_params=pltpu.CompilerParams(vmem_limit_bytes=1 << 20),
    )(*sources)
    both = ("omega", "row")
    return (lax.ppermute(z1, both, row_pairs(ring, column, 0)), lax.ppermute(z2, both, row_pairs(ring, column, 1)))


def row_pairs(ring, column, start):
    pairs = []
    for i in range(ring):
        for r in range(column):
            mate = r + 1 if (r - start) % 2 == 0 else r - 1
            there = (i, mate) if 0 <= mate < column else (i ^ 1, r)
            pairs.append((i * column + r, there[0] * column + there[1]))
    return pairs


def steps(frames, thresholds, spot_boxes):
    count, rows, columns = frames.shape
    slots = spot_boxes.shape[1]
    early = count - REACH
    strips = columns // LANES
    ring = lax.axis_size("omega")
    partner = [(i, i ^ 1) for i in range(ring)]
    other = [(i, (i - 1) % ring if i % 2 == 0 else (i + 1) % ring) for i in range(ring)]

    in_hbm = pltpu.with_memory_space_constraint(frames, pltpu.HBM)
    small = pltpu.CompilerParams(vmem_limit_bytes=1 << 20)
    edges = pl.pallas_call(
        edge_kernel,
        out_shape=shape(REACH, 2 * SUB, columns),
        in_specs=[hbm()],
        out_specs=vmem(),
        scratch_shapes=[pltpu.SemaphoreType.DMA((2,))],
        compiler_params=small,
        name="edge",
    )(in_hbm)
    b0 = lax.ppermute(edges, "omega", other)
    near, *pieces = pl.pallas_call(
        pack_kernel,
        out_shape=(shape(REACH, rows, columns),)
        + tuple(shape(end - begin, rows - 2 * SUB, columns) for begin, end in PIECES),
        in_specs=[hbm()],
        out_specs=(vmem(),) * (1 + len(PIECES)),
        scratch_shapes=[pltpu.SemaphoreType.DMA((1 + len(PIECES),))],
        compiler_params=small,
        name="pack",
    )(in_hbm)
    a = lax.ppermute(near, "omega", partner)
    pieces = [lax.ppermute(piece, "omega", other) for piece in pieces]
    z1, z2 = row_exchange([frames, a], strips)
    far1, far2 = row_exchange([b0], strips)

    level = jnp.broadcast_to((thresholds.astype(jnp.float32) / 64.0)[:, None], (rows, LANES))
    boxes = jnp.concatenate([spot_boxes, spot_boxes], axis=1)

    padded = rows + 2 * TOP
    weight, part, edge, sums, sel = pl.pallas_call(
        functools.partial(early_kernel, early=early),
        out_shape=(
            shape(count, rows, columns),
            shape(REACH, strips, rows + SUB, LANES),
            shape(2, strips, padded, LANES),
            shape(3, 2 * slots),
            jax.ShapeDtypeStruct((columns, 2 * slots), jnp.bfloat16),
        ),
        in_specs=[vmem()] * 6,
        out_specs=(hbm(), vmem(), vmem(), vmem(), vmem()),
        scratch_shapes=[
            pltpu.VMEM((early + 2, strips, padded, LANES), jnp.float32),
            pltpu.VMEM((early + 2, strips, padded, LANES), jnp.float32),
            pltpu.VMEM((early, rows, columns), jnp.float32),
            pltpu.SemaphoreType.DMA((2,)),
        ],
        compiler_params=pltpu.CompilerParams(vmem_limit_bytes=14 << 20),
        cost_estimate=pl.CostEstimate(flops=40 * frames.size, bytes_accessed=16 << 20, transcendentals=0),
        name="early",
    )(frames, a, z1, z2, level, boxes)
    edge = [edge]
    for (begin, end), piece in zip(PIECES, pieces):
        final = end == REACH
        ahead = end == REACH - 1
        late = end - begin
        handed = (shape(4, slots),)
        if not final:
            edges = (shape(strips, padded, LANES), shape(strips, rows, LANES)) if ahead else (shape(2, strips, padded, LANES),)
            handed = (shape(REACH - end, strips, rows + SUB, LANES), *edges, shape(3, 2 * slots))
        weight, *rest = pl.pallas_call(
            functools.partial(late_kernel, count=count, piece=(begin, end)),
            out_shape=(shape(count, rows, columns), *handed),
            in_specs=[vmem()] * (9 + len(edge)) + [hbm()],
            out_specs=(hbm(),) + (vmem(),) * len(handed),
            input_output_aliases={9 + len(edge): 0},
            scratch_shapes=[
                pltpu.VMEM((late, strips, padded, LANES), jnp.float32),
                pltpu.VMEM((late, strips, padded, LANES), jnp.float32),
                pltpu.VMEM((late, rows, columns), jnp.float32),
                pltpu.SemaphoreType.DMA((2,)),
            ],
            compiler_params=pltpu.CompilerParams(vmem_limit_bytes=14 << 20),
            cost_estimate=pl.CostEstimate(flops=8 * late * rows * columns, bytes_accessed=4 << 20, transcendentals=0),
        )(part, piece, b0, far1, far2, level, sel, boxes, sums, *edge, weight)
        if final:
            (stats,) = rest
        else:
            part, *edge, sums = rest
    return weight, stats


def solution(mesh):
    return jax.shard_map(
        steps,
        mesh=mesh,
        in_specs=(P("omega", "row", None), P("row"), P(None, ("omega", "row"))),
        out_specs=(P("omega", "row", None), P(None, ("omega", "row"))),
        check_vma=False,
    )
```

```python
import functools

import jax
import jax.numpy as jnp
from jax import lax
from jax.experimental import pallas as pl
from jax.experimental.pallas import tpu as pltpu
from jax.sharding import PartitionSpec as P


BW = 4
BOX_F = 8
BOX_R = 16
BOX_C = 16
SHARP = 8.0

SUB = 8
LANES = 128
REACH = BW + 2
SPAN = 2 * BW + 1
NEG = -1e30
ZPAD = 6
TOP = 8
PIECES = ((0, 4), (4, 5), (5, 6))
SCALE = 1.0 / (SPAN * 64.0)


def frame_taps():
    three = {-1: 1, 0: 2, 1: 1}
    return [
        SPAN * three.get(d, 0) - sum(w for e, w in three.items() if abs(d - e) <= BW) for d in range(BW + 2)
    ]


def next_column(strips, lane, edge):
    rolled = [pltpu.roll(v, LANES - 1, 1) for v in strips] + [edge]
    return [jnp.where(lane == LANES - 1, rolled[j + 1], rolled[j]) for j in range(len(strips))]


def previous_column(strips, lane, edge):
    rolled = [edge] + [pltpu.roll(v, 1, 1) for v in strips]
    return [jnp.where(lane == 0, rolled[j], rolled[j + 1]) for j in range(len(strips))]


def column_tops(strips, lane):
    tops = [jnp.maximum(a, b) for a, b in zip(strips, next_column(strips, lane, strips[-1]))]
    return [jnp.maximum(a, b) for a, b in zip(tops, previous_column(tops, lane, tops[0]))]


def iotas():
    sub = lax.broadcasted_iota(jnp.int32, (SUB, LANES), 0)
    lane = lax.broadcasted_iota(jnp.int32, (SUB, LANES), 1)
    return sub, lane


def is_even():
    return lax.rem(lax.axis_index("omega"), 2) == 0


def row_is_even():
    return lax.rem(lax.axis_index("row"), 2) == 0


def rows_of(t):
    return pl.ds(t * SUB, SUB)


def store_rows(ref, i, j, tiles):
    for t, v in enumerate(tiles[:-1]):
        ref[i, j, pl.ds(TOP + t * SUB, SUB), :] = v
    ref[i, j, pl.ds(0, SUB), :] = tiles[-1]
    ref[i, j, pl.ds(TOP + (len(tiles) - 1) * SUB, SUB), :] = tiles[-1]


def window_starts(rows):
    return [-1 + SUB * k for k in range(rows // SUB)] + [rows + 1 - SUB]


def smooth_window(first, i, smooth, o, start, rows, strips):
    sub, lane = iotas()
    place = lax.axis_index("row")
    zero = jnp.zeros((SUB, LANES), jnp.float32)
    seconds = []
    for j in range(strips):
        a, b, c = (first[i, j, pl.ds(TOP + start + e, SUB), :] for e in (-1, 0, 1))
        seconds.append((a + b) + (b + c))
    pairs = [a + b for a, b in zip(seconds, next_column(seconds, lane, zero))]
    sums = [a + b for a, b in zip(pairs, previous_column(pairs, lane, seconds[0]))]
    for j in range(strips):
        v = sums[j]
        if start < 0:
            v = jnp.where((sub == 0) & (place == 0), NEG, v)
        if start + SUB > rows:
            v = jnp.where((sub == SUB - 1) & (place == lax.axis_size("row") - 1), NEG, v)
        smooth[o, j, pl.ds(TOP + start, SUB), :] = v


def smooth_stage(first, smooth, count, shift, rows, strips):
    def body(i, carry):
        for start in window_starts(rows):
            smooth_window(first, i, smooth, i + shift, start, rows, strips)
        return carry

    lax.fori_loop(0, count, body, 0)


def row_tops(ref, i, base, strips):
    loads = ([ref[i, j, pl.ds(base + e, SUB), :] for e in (-1, 0, 1)] for j in range(strips))
    return [jnp.maximum(jnp.maximum(a, b), c) for a, b, c in loads]


def weight_of(s, top, floor):
    return jnp.exp((SHARP * SCALE) * (s - top)) * jnp.maximum(s * SCALE - floor, 0.0)


def weigh(smooth_of, level, weight, place, count, rows, strips, tail=None):
    _, lane = iotas()

    def body(t, carry):
        base = t * SUB + TOP
        at = pl.ds(pl.multiple_of(t * SUB, SUB), SUB)
        tops_of = lambda i: row_tops(*smooth_of(i), base, strips)
        here = tops_of(1)
        before = [jnp.maximum(a, b) for a, b in zip(tops_of(0), here)]
        floor = level[at, :]
        for i in range(1, count + 1):
            after = tops_of(i + 1)
            pairs = [jnp.maximum(a, b) for a, b in zip(here, after)]
            highs = [jnp.maximum(a, b) for a, b in zip(before, pairs)]
            here, before = after, pairs
            tops = column_tops(highs, lane)
            ref, index = smooth_of(i)
            for j in range(strips):
                s = ref[index, j, pl.ds(base, SUB), :]
                weight[place(i), at, pl.ds(j * LANES, LANES)] = weight_of(s, tops[j], floor)
        if tail is not None:
            for j, v in enumerate(column_tops(before, lane)):
                tail[j, at, :] = v
        return carry

    lax.fori_loop(0, rows // SUB, body, 0)


def weigh_last(first, smooth, centre, tail, level, weight, rows, strips):
    _, lane = iotas()
    for k, start in enumerate(window_starts(rows)):
        smooth_window(first, 0, smooth, 0, start, rows, strips)
        if k == 0:
            continue
        t = k - 1
        base = t * SUB + TOP
        at = pl.ds(t * SUB, SUB)
        tops = column_tops(row_tops(smooth, 0, base, strips), lane)
        floor = level[at, :]
        for j in range(strips):
            s = centre[j, pl.ds(base, SUB), :]
            top = jnp.maximum(tops[j], tail[j, at, :])
            weight[0, at, pl.ds(j * LANES, LANES)] = weight_of(s, top, floor)


def box_sums(weight, sel, boxes, first, frames, start):
    count, rows, columns = weight.shape
    group = 2 if count % 2 == 0 else 1
    slots2 = sel.shape[1]
    frame_base = lax.axis_index("omega") * frames
    live = boxes[0:1, :] >= 0
    f0 = jnp.where(live, boxes[0:1, :] - frame_base, -BOX_F - frames)
    r0 = boxes[1:2, :] - lax.axis_index("row") * rows
    row = lax.broadcasted_iota(jnp.int32, (rows, slots2), 0) - r0
    row_pick = jnp.where((row >= 0) & (row < BOX_R), 1.0, 0.0)
    row_odd = row_pick * (2 * row - (BOX_R - 1)).astype(jnp.float32)

    def body(i, carry):
        w = weight[pl.ds(i * group, group)].reshape(group * rows, columns)
        high = w.astype(jnp.bfloat16)
        low = (w - high.astype(jnp.float32)).astype(jnp.bfloat16)
        table = sel[...]
        folded = jnp.dot(high, table, preferred_element_type=jnp.float32)
        folded = folded + jnp.dot(low, table, preferred_element_type=jnp.float32)
        for k in range(group):
            part = folded[k * rows : (k + 1) * rows]
            frame = first + i * group + k - f0
            pick = jnp.where((frame >= 0) & (frame < BOX_F), 1.0, 0.0)
            odd = pick * (2 * frame - (BOX_F - 1)).astype(jnp.float32)
            plain = jnp.sum(part * row_pick, axis=0, keepdims=True)
            by_row = jnp.sum(part * row_odd, axis=0, keepdims=True)
            carry = (carry[0] + plain * pick, carry[1] + plain * odd, carry[2] + by_row * pick)
        return carry

    return lax.fori_loop(0, count // group, body, start)


def halo_tile(z1, z2, index, j):
    sub, _ = iotas()
    even = row_is_even()
    shift1 = jnp.where(even, ZPAD, 0)
    head = (sub < SUB // 2) == even
    one = z1[j, pl.ds(2 * index + shift1, SUB), :]
    two = z2[j, pl.ds(2 * index + ZPAD - shift1, SUB), :]
    place = lax.axis_index("row")
    inside = (sub >= SUB // 2) | (place != lax.axis_size("row") - 1)
    inside = inside & ((sub < SUB // 2) | (place != 0))
    return jnp.where(inside, jnp.where(head, one, two), 0.0)


def edge_kernel(x, b0, sems):
    count, rows, _ = x.shape
    start = jnp.where(is_even(), 0, count - REACH)
    copies = [
        pltpu.make_async_copy(x.at[pl.ds(start, REACH), pl.ds(row, SUB)], b0.at[:, pl.ds(to, SUB)], sems.at[k])
        for k, (row, to) in enumerate(((0, 0), (rows - SUB, SUB)))
    ]
    for copy in copies:
        copy.start()
    for copy in copies:
        copy.wait()


def pack_kernel(x, near, *rest):
    count, rows, _ = x.shape
    *pieces, sems = rest
    even = is_even()
    copies = [pltpu.make_async_copy(x.at[pl.ds(jnp.where(even, count - REACH, 0), REACH)], near, sems.at[0])]
    for k, (begin, end) in enumerate(PIECES):
        start = jnp.where(even, begin, count - end)
        source = x.at[pl.ds(start, end - begin), pl.ds(SUB, rows - 2 * SUB)]
        copies.append(pltpu.make_async_copy(source, pieces[k], sems.at[k + 1]))
    for copy in copies:
        copy.start()
    for copy in copies:
        copy.wait()


def rows_kernel(*refs):
    *sources, z1, z2 = refs
    _, _ = iotas()
    even = row_is_even()
    strips = z1.shape[0]
    for j in range(strips):
        at = pl.ds(j * LANES, LANES)
        k = ZPAD
        for z in (z1, z2):
            z[j, 0:SUB, :] = jnp.zeros((SUB, LANES), jnp.float32)
            z[j, pl.ds(z.shape[1] - SUB, SUB), :] = jnp.zeros((SUB, LANES), jnp.float32)
        for source in sources:
            rows = source.shape[1]
            for i in range(source.shape[0]):
                upper, lower = source[i, 0:2, at], source[i, rows - 2 : rows, at]
                z1[j, k : k + 2, :] = jnp.where(even, lower, upper)
                z2[j, k : k + 2, :] = jnp.where(even, upper, lower)
                k += 2


def table_kernel(boxes, sel):
    slots = boxes.shape[1] // 2
    step = lax.broadcasted_iota(jnp.int32, sel.shape, 0) - boxes[2:3, :]
    odd = lax.broadcasted_iota(jnp.int32, sel.shape, 1) >= slots
    value = jnp.where(odd, 2 * step - (BOX_C - 1), 1).astype(jnp.float32)
    inside = (step >= 0) & (step < BOX_C) & (boxes[0:1, :] >= 0)
    sel[...] = jnp.where(inside, value, 0.0).astype(jnp.bfloat16)


def early_kernel(
    x, a, z1, z2, level, sel, boxes, out, part, edge, sums, first, smooth, weight, sems, *, early
):
    count, rows, columns = x.shape
    tiles, strips = rows // SUB, columns // LANES
    even = is_even()

    def body(j, carry):
        at = pl.ds(pl.multiple_of(j * LANES, LANES), LANES)

        def load(p):
            if p >= count:
                return None
            if p < 0:
                index = jnp.where(even, -1 - p, REACH + p)
                return [a[index, rows_of(t), at] for t in range(tiles)] + [halo_tile(z1, z2, count + index, j)]
            index = jnp.where(even, count - 1 - p, p)
            return [x[index, rows_of(t), at] for t in range(tiles)] + [halo_tile(z1, z2, index, j)]

        window = load(-REACH)
        for p in range(1 - REACH, SPAN - REACH):
            window = [u + v for u, v in zip(window, load(p))]
        last_c = last_d = None
        for p in range(-2, count + 2):
            if p > -2:
                if p + BW < count:
                    window = [u + v for u, v in zip(window, load(p + BW))]
                window = [u - v for u, v in zip(window, load(p - BW - 1))]
            f = load(p)
            c = [-v for v in window] if f is None else [float(SPAN) * u - v for u, v in zip(f, window)]
            if last_c is not None:
                d = [u + v for u, v in zip(last_c, c)]
                if last_d is not None:
                    result = [u + v for u, v in zip(last_d, d)]
                    q = p - 1
                    if q <= early:
                        store_rows(first, q + 1, j, result)
                    else:
                        for t, v in enumerate(result):
                            part[q - early - 1, j, rows_of(t), :] = v
                last_d = d
            last_c = c
        return carry

    lax.fori_loop(0, strips, body, 0)
    smooth_stage(first, smooth, early + 2, 0, rows, strips)
    copy_edge = pltpu.make_async_copy(smooth.at[pl.ds(early, 2)], edge, sems.at[0])
    copy_edge.start()
    weigh(lambda i: (smooth, i), level, weight, lambda i: jnp.where(even, early - i, i - 1), early, rows, strips)
    start = jnp.where(even, count - early, 0)
    copy = pltpu.make_async_copy(weight, out.at[pl.ds(start, early)], sems.at[1])
    copy.start()
    zero = jnp.zeros((1, sel.shape[1]), jnp.float32)
    result = box_sums(weight, sel, boxes, start, count, (zero,) * 3)
    for i in range(3):
        sums[i : i + 1, :] = result[i]
    copy_edge.wait()
    copy.wait()


def late_kernel(part, b, b0, z1, z2, level, sel, boxes, sums, *rest, count, piece):
    begin, end = piece
    late = end - begin
    final = end == REACH
    ahead = end == REACH - 1
    if final:
        edge, tail, _, out, *rest = rest
    else:
        edge, _, out, *rest = rest
    if final:
        stats, first, smooth, weight, sems, figures = rest
    elif ahead:
        new_part, new_edge, tail, new_sums, first, smooth, weight, sems = rest
    else:
        new_part, new_edge, new_sums, first, smooth, weight, sems = rest
    rows, columns = out.shape[1], out.shape[2]
    tiles, strips = rows // SUB, columns // LANES
    even = is_even()
    taps = frame_taps()
    early = count - REACH

    def body(j, carry):
        at = pl.ds(j * LANES if final else pl.multiple_of(j * LANES, LANES), LANES)

        def load(q):
            index = jnp.where(even, end - 1 - q, q - begin)
            where = jnp.where(even, REACH - 1 - q, q)
            return (
                [b0[where, rows_of(0), at]]
                + [b[index, rows_of(t), at] for t in range(tiles - 2)]
                + [b0[where, rows_of(1), at], halo_tile(z1, z2, where, j)]
            )

        fresh = {q: load(q) for q in range(begin, end)}
        for i in range(REACH - begin):
            total = [part[i, j, rows_of(t), :] for t in range(tiles + 1)]
            for q in range(begin, end):
                distance = REACH - 1 + q - begin - i
                if abs(distance) < REACH:
                    tap = float(taps[abs(distance)])
                    if tap == -1.0:
                        total = [u - v for u, v in zip(total, fresh[q])]
                    else:
                        total = [u + tap * v for u, v in zip(total, fresh[q])]
            if i < late:
                store_rows(first, i, j, total)
            else:
                for t, v in enumerate(total):
                    new_part[i - late, j, rows_of(t), :] = v
        return carry

    if final:
        for j in range(strips):
            body(j, 0)
    else:
        lax.fori_loop(0, strips, body, 0)
    copies = []
    if final:
        weigh_last(first, smooth, edge, tail, level, weight, rows, strips)
    else:
        smooth_stage(first, smooth, late, 0, rows, strips)
        if ahead:
            copies.append(pltpu.make_async_copy(smooth.at[late - 1], new_edge, sems.at[0]))
        else:
            copies.append(pltpu.make_async_copy(smooth.at[pl.ds(late - 2, 2)], new_edge, sems.at[0]))
        copies[0].start()
        weigh(
            lambda i: (edge, i) if i < 2 else (smooth, i - 2),
            level,
            weight,
            lambda i: jnp.where(even, late - i, i - 1),
            late,
            rows,
            strips,
            tail if ahead else None,
        )
    place = jnp.where(even, REACH - end, early + begin)
    copies.append(pltpu.make_async_copy(weight, out.at[pl.ds(place, late)], sems.at[1]))
    copies[-1].start()
    start = tuple(sums[i : i + 1, :] for i in range(3))
    total, by_frame, by_row = box_sums(weight, sel, boxes, place, count, start)
    if final:
        slots = stats.shape[1]
        cells = float(BOX_F * BOX_R * BOX_C)
        figures[0:1, :] = total[:, :slots] / cells
        figures[1:2, :] = by_frame[:, :slots] / (cells * (BOX_F - 1))
        figures[2:3, :] = by_row[:, :slots] / (cells * (BOX_R - 1))
        figures[3:4, :] = total[:, slots:] / (cells * (BOX_C - 1))
        copies.append(pltpu.make_async_copy(figures, stats, sems.at[0]))
        copies[-1].start()
    else:
        for i, v in enumerate((total, by_frame, by_row)):
            new_sums[i : i + 1, :] = v
    for copy in copies:
        copy.wait()


def shape(*sizes):
    return jax.ShapeDtypeStruct(sizes, jnp.float32)


def vmem():
    return pl.BlockSpec(memory_space=pltpu.VMEM)


def hbm():
    return pl.BlockSpec(memory_space=pltpu.HBM)


def row_exchange(sources, strips):
    ring, column = lax.axis_size("omega"), lax.axis_size("row")
    frames = sum(v.shape[0] for v in sources)
    rows = shape(strips, 2 * frames + 2 * ZPAD, LANES)
    z1, z2 = pl.pallas_call(
        rows_kernel,
        out_shape=(rows, rows),
        in_specs=[vmem()] * len(sources),
        out_specs=(vmem(), vmem()),
        compiler_params=pltpu.CompilerParams(vmem_limit_bytes=1 << 20),
    )(*sources)
    both = ("omega", "row")
    return (lax.ppermute(z1, both, row_pairs(ring, column, 0)), lax.ppermute(z2, both, row_pairs(ring, column, 1)))


def row_pairs(ring, column, start):
    pairs = []
    for i in range(ring):
        for r in range(column):
            mate = r + 1 if (r - start) % 2 == 0 else r - 1
            there = (i, mate) if 0 <= mate < column else (i ^ 1, r)
            pairs.append((i * column + r, there[0] * column + there[1]))
    return pairs


def steps(frames, thresholds, spot_boxes):
    count, rows, columns = frames.shape
    slots = spot_boxes.shape[1]
    early = count - REACH
    strips = columns // LANES
    ring = lax.axis_size("omega")
    partner = [(i, i ^ 1) for i in range(ring)]
    other = [(i, (i - 1) % ring if i % 2 == 0 else (i + 1) % ring) for i in range(ring)]

    in_hbm = pltpu.with_memory_space_constraint(frames, pltpu.HBM)
    small = pltpu.CompilerParams(vmem_limit_bytes=1 << 20)
    edges = pl.pallas_call(
        edge_kernel,
        out_shape=shape(REACH, 2 * SUB, columns),
        in_specs=[hbm()],
        out_specs=vmem(),
        scratch_shapes=[pltpu.SemaphoreType.DMA((2,))],
        compiler_params=small,
        name="edge",
    )(in_hbm)
    b0 = lax.ppermute(edges, "omega", other)
    near, *pieces = pl.pallas_call(
        pack_kernel,
        out_shape=(shape(REACH, rows, columns),)
        + tuple(shape(end - begin, rows - 2 * SUB, columns) for begin, end in PIECES),
        in_specs=[hbm()],
        out_specs=(vmem(),) * (1 + len(PIECES)),
        scratch_shapes=[pltpu.SemaphoreType.DMA((1 + len(PIECES),))],
        compiler_params=small,
        name="pack",
    )(in_hbm)
    a = lax.ppermute(near, "omega", partner)
    pieces = [lax.ppermute(piece, "omega", other) for piece in pieces]
    z1, z2 = row_exchange([frames, a], strips)
    far1, far2 = row_exchange([b0], strips)

    level = jnp.broadcast_to((thresholds.astype(jnp.float32) / 64.0)[:, None], (rows, LANES))
    boxes = jnp.concatenate([spot_boxes, spot_boxes], axis=1)

    padded = rows + 2 * TOP
    sel = pl.pallas_call(
        table_kernel,
        out_shape=jax.ShapeDtypeStruct((columns, 2 * slots), jnp.bfloat16),
        in_specs=[vmem()],
        out_specs=vmem(),
        compiler_params=small,
        name="table",
    )(boxes)
    weight, part, edge, sums = pl.pallas_call(
        functools.partial(early_kernel, early=early),
        out_shape=(
            shape(count, rows, columns),
            shape(REACH, strips, rows + SUB, LANES),
            shape(2, strips, padded, LANES),
            shape(3, 2 * slots),
        ),
        in_specs=[vmem()] * 7,
        out_specs=(hbm(), vmem(), vmem(), vmem()),
        scratch_shapes=[
            pltpu.VMEM((early + 2, strips, padded, LANES), jnp.float32),
            pltpu.VMEM((early + 2, strips, padded, LANES), jnp.float32),
            pltpu.VMEM((early, rows, columns), jnp.float32),
            pltpu.SemaphoreType.DMA((2,)),
        ],
        compiler_params=pltpu.CompilerParams(vmem_limit_bytes=14 << 20),
        cost_estimate=pl.CostEstimate(flops=40 * frames.size, bytes_accessed=16 << 20, transcendentals=0),
        name="early",
    )(frames, a, z1, z2, level, sel, boxes)
    edge = [edge]
    for (begin, end), piece in zip(PIECES, pieces):
        final = end == REACH
        ahead = end == REACH - 1
        late = end - begin
        handed = (shape(4, slots),)
        if not final:
            edges = (shape(strips, padded, LANES), shape(strips, rows, LANES)) if ahead else (shape(2, strips, padded, LANES),)
            handed = (shape(REACH - end, strips, rows + SUB, LANES), *edges, shape(3, 2 * slots))
        weight, *rest = pl.pallas_call(
            functools.partial(late_kernel, count=count, piece=(begin, end)),
            out_shape=(shape(count, rows, columns), *handed),
            in_specs=[vmem()] * (9 + len(edge)) + [hbm()],
            out_specs=(hbm(),) + (hbm() if final else vmem(),) * len(handed),
            input_output_aliases={9 + len(edge): 0},
            scratch_shapes=[
                pltpu.VMEM((late, strips, padded, LANES), jnp.float32),
                pltpu.VMEM((late, strips, padded, LANES), jnp.float32),
                pltpu.VMEM((late, rows, columns), jnp.float32),
                pltpu.SemaphoreType.DMA((2,)),
            ]
            + ([pltpu.VMEM((4, slots), jnp.float32)] if final else []),
            compiler_params=pltpu.CompilerParams(vmem_limit_bytes=14 << 20),
            cost_estimate=pl.CostEstimate(flops=8 * late * rows * columns, bytes_accessed=4 << 20, transcendentals=0),
        )(part, piece, b0, far1, far2, level, sel, boxes, sums, *edge, weight)
        if final:
            (stats,) = rest
        else:
            part, *edge, sums = rest
    return weight, stats


def solution(mesh):
    return jax.shard_map(
        steps,
        mesh=mesh,
        in_specs=(P("omega", "row", None), P("row"), P(None, ("omega", "row"))),
        out_specs=(P("omega", "row", None), P(None, ("omega", "row"))),
        check_vma=False,
    )
```

```python
import functools

import jax
import jax.numpy as jnp
from jax import lax
from jax.experimental import pallas as pl
from jax.experimental.pallas import tpu as pltpu
from jax.sharding import PartitionSpec as P


BW = 4
BOX_F = 8
BOX_R = 16
BOX_C = 16
SHARP = 8.0

SUB = 8
LANES = 128
REACH = BW + 2
SPAN = 2 * BW + 1
NEG = -1e30
ZPAD = 6
TOP = 8
PIECES = ((0, 4), (4, 5), (5, 6))
SCALE = 1.0 / (SPAN * 64.0)


def frame_taps():
    three = {-1: 1, 0: 2, 1: 1}
    return [
        SPAN * three.get(d, 0) - sum(w for e, w in three.items() if abs(d - e) <= BW) for d in range(BW + 2)
    ]


def next_column(strips, lane, edge):
    rolled = [pltpu.roll(v, LANES - 1, 1) for v in strips] + [edge]
    return [jnp.where(lane == LANES - 1, rolled[j + 1], rolled[j]) for j in range(len(strips))]


def previous_column(strips, lane, edge):
    rolled = [edge] + [pltpu.roll(v, 1, 1) for v in strips]
    return [jnp.where(lane == 0, rolled[j], rolled[j + 1]) for j in range(len(strips))]


def column_sums(strips, lane):
    pairs = [a + b for a, b in zip(strips, next_column(strips, lane, jnp.zeros_like(strips[0])))]
    return [a + b for a, b in zip(pairs, previous_column(pairs, lane, strips[0]))]


def column_tops(strips, lane):
    tops = [jnp.maximum(a, b) for a, b in zip(strips, next_column(strips, lane, strips[-1]))]
    return [jnp.maximum(a, b) for a, b in zip(tops, previous_column(tops, lane, tops[0]))]


def iotas():
    sub = lax.broadcasted_iota(jnp.int32, (SUB, LANES), 0)
    lane = lax.broadcasted_iota(jnp.int32, (SUB, LANES), 1)
    return sub, lane


def is_even():
    return lax.rem(lax.axis_index("omega"), 2) == 0


def row_is_even():
    return lax.rem(lax.axis_index("row"), 2) == 0


def rows_of(t):
    return pl.ds(t * SUB, SUB)


def store_rows(ref, i, j, tiles):
    for t, v in enumerate(tiles[:-1]):
        ref[i, j, pl.ds(TOP + t * SUB, SUB), :] = v
    ref[i, j, pl.ds(0, SUB), :] = tiles[-1]
    ref[i, j, pl.ds(TOP + (len(tiles) - 1) * SUB, SUB), :] = tiles[-1]


def window_starts(rows):
    return [-1 + SUB * k for k in range(rows // SUB)] + [rows + 1 - SUB]


def smooth_window(first, i, smooth, o, start, rows, strips):
    sub, lane = iotas()
    place = lax.axis_index("row")
    seconds = []
    for j in range(strips):
        a, b, c = (first[i, j, pl.ds(TOP + start + e, SUB), :] for e in (-1, 0, 1))
        seconds.append((a + b) + (b + c))
    sums = column_sums(seconds, lane)
    for j in range(strips):
        v = sums[j]
        if start < 0:
            v = jnp.where((sub == 0) & (place == 0), NEG, v)
        if start + SUB > rows:
            v = jnp.where((sub == SUB - 1) & (place == lax.axis_size("row") - 1), NEG, v)
        smooth[o, j, pl.ds(TOP + start, SUB), :] = v


def smooth_stage(first, smooth, count, shift, rows, strips):
    def body(i, carry):
        for start in window_starts(rows):
            smooth_window(first, i, smooth, i + shift, start, rows, strips)
        return carry

    lax.fori_loop(0, count, body, 0)


def row_tops(ref, i, base, strips):
    loads = ([ref[i, j, pl.ds(base + e, SUB), :] for e in (-1, 0, 1)] for j in range(strips))
    return [jnp.maximum(jnp.maximum(a, b), c) for a, b, c in loads]


def weight_of(s, top, floor):
    return jnp.exp((SHARP * SCALE) * (s - top)) * jnp.maximum(s * SCALE - floor, 0.0)


def weigh(smooth_of, level, weight, place, count, rows, strips, tail=None):
    _, lane = iotas()

    def body(t, carry):
        base = t * SUB + TOP
        at = pl.ds(pl.multiple_of(t * SUB, SUB), SUB)
        tops_of = lambda i: row_tops(*smooth_of(i), base, strips)
        here = tops_of(1)
        before = [jnp.maximum(a, b) for a, b in zip(tops_of(0), here)]
        floor = level[at, :]
        for i in range(1, count + 1):
            after = tops_of(i + 1)
            pairs = [jnp.maximum(a, b) for a, b in zip(here, after)]
            highs = [jnp.maximum(a, b) for a, b in zip(before, pairs)]
            here, before = after, pairs
            tops = column_tops(highs, lane)
            ref, index = smooth_of(i)
            for j in range(strips):
                s = ref[index, j, pl.ds(base, SUB), :]
                weight[place(i), at, pl.ds(j * LANES, LANES)] = weight_of(s, tops[j], floor)
        if tail is not None:
            for j, v in enumerate(column_tops(before, lane)):
                tail[j, at, :] = v
        return carry

    lax.fori_loop(0, rows // SUB, body, 0)


def weigh_last(ready, fresh, padded, smooth, centre, tail, level, weight, rows, strips):
    _, lane = iotas()
    tap = float(frame_taps()[-1])
    starts = window_starts(rows)
    zero = jnp.zeros((SUB, LANES), jnp.float32)
    for j in range(strips):
        for t in range(rows // SUB):
            inner = 0 < t < rows // SUB - 1
            padded[j, pl.ds(TOP + t * SUB, SUB), :] = fresh[j, rows_of(t - 1), :] if inner else zero
    for k, start in enumerate(starts):
        for j in range(strips):
            v = ready[j, pl.ds(TOP + start, SUB), :]
            if 0 < k < len(starts) - 1:
                a, b, c = (padded[j, pl.ds(TOP + start + e, SUB), :] for e in (-1, 0, 1))
                v = v + tap * ((a + b) + (b + c))
            smooth[0, j, pl.ds(TOP + start, SUB), :] = v
        if k == 0:
            continue
        t = k - 1
        base = t * SUB + TOP
        at = pl.ds(t * SUB, SUB)
        tops = column_tops(row_tops(smooth, 0, base, strips), lane)
        floor = level[at, :]
        for j in range(strips):
            s = centre[j, pl.ds(base, SUB), :]
            top = jnp.maximum(tops[j], tail[j, at, :])
            weight[0, at, pl.ds(j * LANES, LANES)] = weight_of(s, top, floor)


def box_sums(weight, sel, boxes, first, frames, start):
    count, rows, columns = weight.shape
    group = 2 if count % 2 == 0 else 1
    slots2 = sel.shape[1]
    frame_base = lax.axis_index("omega") * frames
    live = boxes[0:1, :] >= 0
    f0 = jnp.where(live, boxes[0:1, :] - frame_base, -BOX_F - frames)
    r0 = boxes[1:2, :] - lax.axis_index("row") * rows
    row = lax.broadcasted_iota(jnp.int32, (rows, slots2), 0) - r0
    row_pick = jnp.where((row >= 0) & (row < BOX_R), 1.0, 0.0)
    row_odd = row_pick * (2 * row - (BOX_R - 1)).astype(jnp.float32)

    def body(i, carry):
        w = weight[pl.ds(i * group, group)].reshape(group * rows, columns)
        high = w.astype(jnp.bfloat16)
        low = (w - high.astype(jnp.float32)).astype(jnp.bfloat16)
        table = sel[...]
        folded = jnp.dot(high, table, preferred_element_type=jnp.float32)
        folded = folded + jnp.dot(low, table, preferred_element_type=jnp.float32)
        for k in range(group):
            part = folded[k * rows : (k + 1) * rows]
            frame = first + i * group + k - f0
            pick = jnp.where((frame >= 0) & (frame < BOX_F), 1.0, 0.0)
            odd = pick * (2 * frame - (BOX_F - 1)).astype(jnp.float32)
            plain = jnp.sum(part * row_pick, axis=0, keepdims=True)
            by_row = jnp.sum(part * row_odd, axis=0, keepdims=True)
            carry = (carry[0] + plain * pick, carry[1] + plain * odd, carry[2] + by_row * pick)
        return carry

    return lax.fori_loop(0, count // group, body, start)


def halo_tile(z1, z2, index, j):
    sub, _ = iotas()
    even = row_is_even()
    shift1 = jnp.where(even, ZPAD, 0)
    head = (sub < SUB // 2) == even
    one = z1[j, pl.ds(2 * index + shift1, SUB), :]
    two = z2[j, pl.ds(2 * index + ZPAD - shift1, SUB), :]
    place = lax.axis_index("row")
    inside = (sub >= SUB // 2) | (place != lax.axis_size("row") - 1)
    inside = inside & ((sub < SUB // 2) | (place != 0))
    return jnp.where(inside, jnp.where(head, one, two), 0.0)


def edge_kernel(x, b0, sems):
    count, rows, _ = x.shape
    start = jnp.where(is_even(), 0, count - REACH)
    copies = [
        pltpu.make_async_copy(x.at[pl.ds(start, REACH), pl.ds(row, SUB)], b0.at[:, pl.ds(to, SUB)], sems.at[k])
        for k, (row, to) in enumerate(((0, 0), (rows - SUB, SUB)))
    ]
    for copy in copies:
        copy.start()
    for copy in copies:
        copy.wait()


def pack_kernel(x, near, rims, *rest):
    count, rows, _ = x.shape
    *pieces, sems = rest
    even = is_even()
    copies = [pltpu.make_async_copy(x.at[pl.ds(jnp.where(even, count - REACH, 0), REACH)], near, sems.at[0])]
    *targets, filtered, last = pieces
    for k, (begin, end) in enumerate(PIECES):
        start = jnp.where(even, begin, count - end)
        source = x.at[pl.ds(start, end - begin), pl.ds(SUB, rows - 2 * SUB)]
        copies.append(pltpu.make_async_copy(source, (*targets, last)[k], sems.at[k + 1]))
    for k, (row, to) in enumerate(((0, 0), (rows - SUB, SUB))):
        copies.append(
            pltpu.make_async_copy(x.at[:, pl.ds(row, SUB)], rims.at[:, pl.ds(to, SUB)], sems.at[len(PIECES) + 1 + k])
        )
    for copy in copies:
        copy.start()
    for copy in copies:
        copy.wait()
    _, lane = iotas()
    strips = filtered.shape[0]
    for t in range(rows // SUB - 2):
        values = [last[0, rows_of(t), pl.ds(j * LANES, LANES)] for j in range(strips)]
        for j, v in enumerate(column_sums(values, lane)):
            filtered[j, rows_of(t), :] = v


def rows_kernel(*refs):
    *sources, z1, z2 = refs
    _, _ = iotas()
    even = row_is_even()
    strips = z1.shape[0]
    for j in range(strips):
        at = pl.ds(j * LANES, LANES)
        k = ZPAD
        for z in (z1, z2):
            z[j, 0:SUB, :] = jnp.zeros((SUB, LANES), jnp.float32)
            z[j, pl.ds(z.shape[1] - SUB, SUB), :] = jnp.zeros((SUB, LANES), jnp.float32)
        for source in sources:
            rows = source.shape[1]
            for i in range(source.shape[0]):
                upper, lower = source[i, 0:2, at], source[i, rows - 2 : rows, at]
                z1[j, k : k + 2, :] = jnp.where(even, lower, upper)
                z2[j, k : k + 2, :] = jnp.where(even, upper, lower)
                k += 2


def table_kernel(boxes, sel):
    slots = boxes.shape[1] // 2
    step = lax.broadcasted_iota(jnp.int32, sel.shape, 0) - boxes[2:3, :]
    odd = lax.broadcasted_iota(jnp.int32, sel.shape, 1) >= slots
    value = jnp.where(odd, 2 * step - (BOX_C - 1), 1).astype(jnp.float32)
    inside = (step >= 0) & (step < BOX_C) & (boxes[0:1, :] >= 0)
    sel[...] = jnp.where(inside, value, 0.0).astype(jnp.bfloat16)


def early_kernel(
    x, a, z1, z2, level, sel, boxes, out, part, edge, sums, first, smooth, weight, sems, *, early
):
    count, rows, columns = x.shape
    tiles, strips = rows // SUB, columns // LANES
    even = is_even()

    def body(j, carry):
        at = pl.ds(pl.multiple_of(j * LANES, LANES), LANES)

        def load(p):
            if p >= count:
                return None
            if p < 0:
                index = jnp.where(even, -1 - p, REACH + p)
                return [a[index, rows_of(t), at] for t in range(tiles)] + [halo_tile(z1, z2, count + index, j)]
            index = jnp.where(even, count - 1 - p, p)
            return [x[index, rows_of(t), at] for t in range(tiles)] + [halo_tile(z1, z2, index, j)]

        window = load(-REACH)
        for p in range(1 - REACH, SPAN - REACH):
            window = [u + v for u, v in zip(window, load(p))]
        last_c = last_d = None
        for p in range(-2, count + 2):
            if p > -2:
                if p + BW < count:
                    window = [u + v for u, v in zip(window, load(p + BW))]
                window = [u - v for u, v in zip(window, load(p - BW - 1))]
            f = load(p)
            c = [-v for v in window] if f is None else [float(SPAN) * u - v for u, v in zip(f, window)]
            if last_c is not None:
                d = [u + v for u, v in zip(last_c, c)]
                if last_d is not None:
                    result = [u + v for u, v in zip(last_d, d)]
                    q = p - 1
                    if q <= early:
                        store_rows(first, q + 1, j, result)
                    else:
                        for t, v in enumerate(result):
                            part[q - early - 1, j, rows_of(t), :] = v
                last_d = d
            last_c = c
        return carry

    lax.fori_loop(0, strips, body, 0)
    smooth_stage(first, smooth, early + 2, 0, rows, strips)
    copy_edge = pltpu.make_async_copy(smooth.at[pl.ds(early, 2)], edge, sems.at[0])
    copy_edge.start()
    weigh(lambda i: (smooth, i), level, weight, lambda i: jnp.where(even, early - i, i - 1), early, rows, strips)
    start = jnp.where(even, count - early, 0)
    copy = pltpu.make_async_copy(weight, out.at[pl.ds(start, early)], sems.at[1])
    copy.start()
    zero = jnp.zeros((1, sel.shape[1]), jnp.float32)
    result = box_sums(weight, sel, boxes, start, count, (zero,) * 3)
    for i in range(3):
        sums[i : i + 1, :] = result[i]
    copy_edge.wait()
    copy.wait()


def late_kernel(part, b, b0, z1, z2, level, sel, boxes, sums, edge, _, out, new_part, *rest, count, piece):
    begin, end = piece
    late = end - begin
    ahead = end == REACH - 1
    new_edge, *tails, new_sums, first, smooth, weight, sems = rest
    rows, columns = out.shape[1], out.shape[2]
    tiles, strips = rows // SUB, columns // LANES
    even = is_even()
    taps = frame_taps()
    early = count - REACH

    def body(j, carry):
        at = pl.ds(pl.multiple_of(j * LANES, LANES), LANES)

        def load_edges(q):
            where = jnp.where(even, REACH - 1 - q, q)
            return b0[where, rows_of(0), at], [b0[where, rows_of(1), at], halo_tile(z1, z2, where, j)]

        def load(q):
            index = jnp.where(even, end - 1 - q, q - begin)
            head, last = load_edges(q)
            return [head] + [b[index, rows_of(t), at] for t in range(tiles - 2)] + last

        def add(total, tap, values):
            if tap == -1.0:
                return [u - v for u, v in zip(total, values)]
            return [u + tap * v for u, v in zip(total, values)]

        fresh = {q: load(q) for q in range(begin, end)}
        for i in range(REACH - begin):
            total = [part[i, j, rows_of(t), :] for t in range(tiles + 1)]
            for q in range(begin, end):
                distance = REACH - 1 + q - begin - i
                if abs(distance) < REACH:
                    total = add(total, float(taps[abs(distance)]), fresh[q])
            if ahead and i == late:
                head, last = load_edges(end)
                tap = float(taps[REACH - 1])
                total = add(total[:1], tap, [head]) + total[1 : tiles - 1] + add(total[tiles - 1 :], tap, last)
            if i < late or ahead:
                store_rows(first, i, j, total)
            else:
                for t, v in enumerate(total):
                    new_part[i - late, j, rows_of(t), :] = v
        return carry

    lax.fori_loop(0, strips, body, 0)
    smooth_stage(first, smooth, late + 1 if ahead else late, 0, rows, strips)
    if ahead:
        copies = [
            pltpu.make_async_copy(smooth.at[late - 1], new_edge, sems.at[0]),
            pltpu.make_async_copy(smooth.at[late], new_part, sems.at[2]),
        ]
    else:
        copies = [pltpu.make_async_copy(smooth.at[pl.ds(late - 2, 2)], new_edge, sems.at[0])]
    for copy in copies:
        copy.start()
    weigh(
        lambda i: (edge, i) if i < 2 else (smooth, i - 2),
        level,
        weight,
        lambda i: jnp.where(even, late - i, i - 1),
        late,
        rows,
        strips,
        *tails,
    )
    place = jnp.where(even, REACH - end, early + begin)
    copies.append(pltpu.make_async_copy(weight, out.at[pl.ds(place, late)], sems.at[1]))
    copies[-1].start()
    start = tuple(sums[i : i + 1, :] for i in range(3))
    for i, v in enumerate(box_sums(weight, sel, boxes, place, count, start)):
        new_sums[i : i + 1, :] = v
    for copy in copies:
        copy.wait()


def last_kernel(ready, fresh, level, sel, boxes, sums, centre, tail, _, out, stats, padded, smooth, weight, figures, sems):
    count, rows, columns = out.shape
    weigh_last(ready, fresh, padded, smooth, centre, tail, level, weight, rows, columns // LANES)
    place = jnp.where(is_even(), 0, count - 1)
    copies = [pltpu.make_async_copy(weight, out.at[pl.ds(place, 1)], sems.at[1])]
    copies[0].start()
    start = tuple(sums[i : i + 1, :] for i in range(3))
    total, by_frame, by_row = box_sums(weight, sel, boxes, place, count, start)
    slots = stats.shape[1]
    cells = float(BOX_F * BOX_R * BOX_C)
    figures[0:1, :] = total[:, :slots] / cells
    figures[1:2, :] = by_frame[:, :slots] / (cells * (BOX_F - 1))
    figures[2:3, :] = by_row[:, :slots] / (cells * (BOX_R - 1))
    figures[3:4, :] = total[:, slots:] / (cells * (BOX_C - 1))
    copies.append(pltpu.make_async_copy(figures, stats, sems.at[0]))
    copies[1].start()
    for copy in copies:
        copy.wait()


def shape(*sizes):
    return jax.ShapeDtypeStruct(sizes, jnp.float32)


def vmem():
    return pl.BlockSpec(memory_space=pltpu.VMEM)


def hbm():
    return pl.BlockSpec(memory_space=pltpu.HBM)


def row_exchange(sources, strips):
    ring, column = lax.axis_size("omega"), lax.axis_size("row")
    frames = sum(v.shape[0] for v in sources)
    rows = shape(strips, 2 * frames + 2 * ZPAD, LANES)
    z1, z2 = pl.pallas_call(
        rows_kernel,
        out_shape=(rows, rows),
        in_specs=[vmem()] * len(sources),
        out_specs=(vmem(), vmem()),
        compiler_params=pltpu.CompilerParams(vmem_limit_bytes=1 << 20),
    )(*sources)
    both = ("omega", "row")
    return (lax.ppermute(z1, both, row_pairs(ring, column, 0)), lax.ppermute(z2, both, row_pairs(ring, column, 1)))


def row_pairs(ring, column, start):
    pairs = []
    for i in range(ring):
        for r in range(column):
            mate = r + 1 if (r - start) % 2 == 0 else r - 1
            there = (i, mate) if 0 <= mate < column else (i ^ 1, r)
            pairs.append((i * column + r, there[0] * column + there[1]))
    return pairs


def steps(frames, thresholds, spot_boxes):
    count, rows, columns = frames.shape
    slots = spot_boxes.shape[1]
    early = count - REACH
    strips = columns // LANES
    ring = lax.axis_size("omega")
    partner = [(i, i ^ 1) for i in range(ring)]
    other = [(i, (i - 1) % ring if i % 2 == 0 else (i + 1) % ring) for i in range(ring)]

    in_hbm = pltpu.with_memory_space_constraint(frames, pltpu.HBM)
    small = pltpu.CompilerParams(vmem_limit_bytes=1 << 20)
    edges = pl.pallas_call(
        edge_kernel,
        out_shape=shape(REACH, 2 * SUB, columns),
        in_specs=[hbm()],
        out_specs=vmem(),
        scratch_shapes=[pltpu.SemaphoreType.DMA((2,))],
        compiler_params=small,
        name="edge",
    )(in_hbm)
    b0 = lax.ppermute(edges, "omega", other)
    near, rims, *pieces = pl.pallas_call(
        pack_kernel,
        out_shape=(shape(REACH, rows, columns), shape(count, 2 * SUB, columns))
        + tuple(shape(end - begin, rows - 2 * SUB, columns) for begin, end in PIECES[:-1])
        + (shape(strips, rows - 2 * SUB, LANES),),
        in_specs=[hbm()],
        out_specs=(vmem(),) * (2 + len(PIECES)),
        scratch_shapes=[
            pltpu.VMEM((1, rows - 2 * SUB, columns), jnp.float32),
            pltpu.SemaphoreType.DMA((3 + len(PIECES),)),
        ],
        compiler_params=small,
        name="pack",
    )(in_hbm)
    a = lax.ppermute(near, "omega", partner)
    pieces = [lax.ppermute(piece, "omega", other) for piece in pieces]
    z1, z2 = row_exchange([rims, a], strips)
    far1, far2 = row_exchange([b0], strips)

    level = jnp.broadcast_to((thresholds.astype(jnp.float32) / 64.0)[:, None], (rows, LANES))
    boxes = jnp.concatenate([spot_boxes, spot_boxes], axis=1)

    padded = rows + 2 * TOP
    sel = pl.pallas_call(
        table_kernel,
        out_shape=jax.ShapeDtypeStruct((columns, 2 * slots), jnp.bfloat16),
        in_specs=[vmem()],
        out_specs=vmem(),
        compiler_params=small,
        name="table",
    )(boxes)
    weight, part, edge, sums = pl.pallas_call(
        functools.partial(early_kernel, early=early),
        out_shape=(
            shape(count, rows, columns),
            shape(REACH, strips, rows + SUB, LANES),
            shape(2, strips, padded, LANES),
            shape(3, 2 * slots),
        ),
        in_specs=[vmem()] * 7,
        out_specs=(hbm(), vmem(), vmem(), vmem()),
        scratch_shapes=[
            pltpu.VMEM((early + 2, strips, padded, LANES), jnp.float32),
            pltpu.VMEM((early + 2, strips, padded, LANES), jnp.float32),
            pltpu.VMEM((early, rows, columns), jnp.float32),
            pltpu.SemaphoreType.DMA((2,)),
        ],
        compiler_params=pltpu.CompilerParams(vmem_limit_bytes=14 << 20),
        cost_estimate=pl.CostEstimate(flops=40 * frames.size, bytes_accessed=16 << 20, transcendentals=0),
        name="early",
    )(frames, a, z1, z2, level, sel, boxes)
    tails = ()
    params = pltpu.CompilerParams(vmem_limit_bytes=14 << 20)
    for (begin, end), piece in zip(PIECES[:-1], pieces[:-1]):
        late = end - begin
        if end == REACH - 1:
            made = late + 1
            handed = (shape(strips, padded, LANES), shape(strips, padded, LANES), shape(strips, rows, LANES))
        else:
            made = late
            handed = (shape(REACH - end, strips, rows + SUB, LANES), shape(2, strips, padded, LANES))
        weight, part, edge, *tails, sums = pl.pallas_call(
            functools.partial(late_kernel, count=count, piece=(begin, end)),
            out_shape=(shape(count, rows, columns), *handed, shape(3, 2 * slots)),
            in_specs=[vmem()] * 10 + [hbm()],
            out_specs=(hbm(),) + (vmem(),) * (1 + len(handed)),
            input_output_aliases={10: 0},
            scratch_shapes=[
                pltpu.VMEM((made, strips, padded, LANES), jnp.float32),
                pltpu.VMEM((made, strips, padded, LANES), jnp.float32),
                pltpu.VMEM((late, rows, columns), jnp.float32),
                pltpu.SemaphoreType.DMA((3,)),
            ],
            compiler_params=params,
            cost_estimate=pl.CostEstimate(flops=8 * late * rows * columns, bytes_accessed=4 << 20, transcendentals=0),
        )(part, piece, b0, far1, far2, level, sel, boxes, sums, edge, weight)
    weight, stats = pl.pallas_call(
        last_kernel,
        out_shape=(shape(count, rows, columns), shape(4, slots)),
        in_specs=[vmem()] * 8 + [hbm()],
        out_specs=(hbm(), hbm()),
        input_output_aliases={8: 0},
        scratch_shapes=[
            pltpu.VMEM((strips, padded, LANES), jnp.float32),
            pltpu.VMEM((1, strips, padded, LANES), jnp.float32),
            pltpu.VMEM((1, rows, columns), jnp.float32),
            pltpu.VMEM((4, slots), jnp.float32),
            pltpu.SemaphoreType.DMA((2,)),
        ],
        compiler_params=params,
        cost_estimate=pl.CostEstimate(flops=8 * rows * columns, bytes_accessed=4 << 20, transcendentals=0),
        name="last",
    )(part, pieces[-1], level, sel, boxes, sums, edge, *tails, weight)
    return weight, stats


def solution(mesh):
    return jax.shard_map(
        steps,
        mesh=mesh,
        in_specs=(P("omega", "row", None), P("row"), P(None, ("omega", "row"))),
        out_specs=(P("omega", "row", None), P(None, ("omega", "row"))),
        check_vma=False,
    )
```

```python
import functools

import jax
import jax.numpy as jnp
from jax import lax
from jax.experimental import pallas as pl
from jax.experimental.pallas import tpu as pltpu
from jax.sharding import PartitionSpec as P


BW = 4
BOX_F = 8
BOX_R = 16
BOX_C = 16
SHARP = 8.0

SUB = 8
LANES = 128
REACH = BW + 2
SPAN = 2 * BW + 1
NEG = -1e30
ZPAD = 6
TOP = 8
PIECES = ((0, 4), (4, 5), (5, 6))
SCALE = 1.0 / (SPAN * 64.0)


def frame_taps():
    three = {-1: 1, 0: 2, 1: 1}
    return [
        SPAN * three.get(d, 0) - sum(w for e, w in three.items() if abs(d - e) <= BW) for d in range(BW + 2)
    ]


def next_column(strips, lane, edge):
    rolled = [pltpu.roll(v, LANES - 1, 1) for v in strips] + [edge]
    return [jnp.where(lane == LANES - 1, rolled[j + 1], rolled[j]) for j in range(len(strips))]


def previous_column(strips, lane, edge):
    rolled = [edge] + [pltpu.roll(v, 1, 1) for v in strips]
    return [jnp.where(lane == 0, rolled[j], rolled[j + 1]) for j in range(len(strips))]


def column_sums(strips, lane):
    pairs = [a + b for a, b in zip(strips, next_column(strips, lane, jnp.zeros_like(strips[0])))]
    return [a + b for a, b in zip(pairs, previous_column(pairs, lane, strips[0]))]


def column_tops(strips, lane):
    tops = [jnp.maximum(a, b) for a, b in zip(strips, next_column(strips, lane, strips[-1]))]
    return [jnp.maximum(a, b) for a, b in zip(tops, previous_column(tops, lane, tops[0]))]


def iotas():
    sub = lax.broadcasted_iota(jnp.int32, (SUB, LANES), 0)
    lane = lax.broadcasted_iota(jnp.int32, (SUB, LANES), 1)
    return sub, lane


def is_even():
    return lax.rem(lax.axis_index("omega"), 2) == 0


def row_is_even():
    return lax.rem(lax.axis_index("row"), 2) == 0


def rows_of(t):
    return pl.ds(t * SUB, SUB)


def store_rows(ref, i, j, tiles):
    for t, v in enumerate(tiles[:-1]):
        ref[i, j, pl.ds(TOP + t * SUB, SUB), :] = v
    ref[i, j, pl.ds(0, SUB), :] = tiles[-1]
    ref[i, j, pl.ds(TOP + (len(tiles) - 1) * SUB, SUB), :] = tiles[-1]


def window_starts(rows):
    return [-1 + SUB * k for k in range(rows // SUB)] + [rows + 1 - SUB]


def smooth_window(first, i, smooth, o, start, rows, strips):
    sub, lane = iotas()
    place = lax.axis_index("row")
    seconds = []
    for j in range(strips):
        a, b, c = (first[i, j, pl.ds(TOP + start + e, SUB), :] for e in (-1, 0, 1))
        seconds.append((a + b) + (b + c))
    sums = column_sums(seconds, lane)
    for j in range(strips):
        v = sums[j]
        if start < 0:
            v = jnp.where((sub == 0) & (place == 0), NEG, v)
        if start + SUB > rows:
            v = jnp.where((sub == SUB - 1) & (place == lax.axis_size("row") - 1), NEG, v)
        smooth[o, j, pl.ds(TOP + start, SUB), :] = v


def smooth_stage(first, smooth, count, shift, rows, strips):
    def body(i, carry):
        for start in window_starts(rows):
            smooth_window(first, i, smooth, i + shift, start, rows, strips)
        return carry

    lax.fori_loop(0, count, body, 0)


def row_tops(ref, i, base, strips):
    loads = ([ref[i, j, pl.ds(base + e, SUB), :] for e in (-1, 0, 1)] for j in range(strips))
    return [jnp.maximum(jnp.maximum(a, b), c) for a, b, c in loads]


def weight_of(s, top, floor):
    return jnp.exp((SHARP * SCALE) * (s - top)) * jnp.maximum(s * SCALE - floor, 0.0)


def weigh(smooth_of, level, weight, place, count, rows, strips, tail=None):
    _, lane = iotas()

    def body(t, carry):
        base = t * SUB + TOP
        at = pl.ds(pl.multiple_of(t * SUB, SUB), SUB)
        tops_of = lambda i: row_tops(*smooth_of(i), base, strips)
        here = tops_of(1)
        before = [jnp.maximum(a, b) for a, b in zip(tops_of(0), here)]
        floor = level[at, :]
        for i in range(1, count + 1):
            after = tops_of(i + 1)
            pairs = [jnp.maximum(a, b) for a, b in zip(here, after)]
            highs = [jnp.maximum(a, b) for a, b in zip(before, pairs)]
            here, before = after, pairs
            tops = column_tops(highs, lane)
            ref, index = smooth_of(i)
            for j in range(strips):
                s = ref[index, j, pl.ds(base, SUB), :]
                weight[place(i), at, pl.ds(j * LANES, LANES)] = weight_of(s, tops[j], floor)
        if tail is not None:
            for j, v in enumerate(column_tops(before, lane)):
                tail[j, at, :] = v
        return carry

    lax.fori_loop(0, rows // SUB, body, 0)


def weigh_last(ready, freshes, padded, smooth, centre, tail, level, weight, rows, strips, first, end):
    _, lane = iotas()
    tap = float(frame_taps()[-1])
    starts = window_starts(rows)
    tiles = rows // SUB
    cut = freshes[0].shape[1] // SUB
    zero = jnp.zeros((SUB, LANES), jnp.float32)
    for j in range(strips):
        for t in range(max(first - 1, 0), min(end + 1, tiles)):
            if t == 0 or t == tiles - 1:
                v = zero
            elif t <= cut:
                v = freshes[0][j, rows_of(t - 1), :]
            else:
                v = freshes[1][j, rows_of(t - 1 - cut), :]
            padded[j, pl.ds(TOP + t * SUB, SUB), :] = v
    for k in range(first, end + 1):
        start = starts[k]
        for j in range(strips):
            v = ready[j, pl.ds(TOP + start, SUB), :]
            if 0 < k < len(starts) - 1:
                a, b, c = (padded[j, pl.ds(TOP + start + e, SUB), :] for e in (-1, 0, 1))
                v = v + tap * ((a + b) + (b + c))
            smooth[0, j, pl.ds(TOP + start, SUB), :] = v
        if k == first:
            continue
        t = k - 1
        base = t * SUB + TOP
        at = pl.ds(t * SUB, SUB)
        tops = column_tops(row_tops(smooth, 0, base, strips), lane)
        floor = level[at, :]
        for j in range(strips):
            s = centre[j, pl.ds(base, SUB), :]
            top = jnp.maximum(tops[j], tail[j, at, :])
            weight[0, rows_of(t - first), pl.ds(j * LANES, LANES)] = weight_of(s, top, floor)


def box_sums(weight, sel, boxes, first, frames, start, top=0, height=None):
    count, rows, columns = weight.shape
    group = 2 if count % 2 == 0 else 1
    slots2 = sel.shape[1]
    frame_base = lax.axis_index("omega") * frames
    live = boxes[0:1, :] >= 0
    f0 = jnp.where(live, boxes[0:1, :] - frame_base, -BOX_F - frames)
    r0 = boxes[1:2, :] - lax.axis_index("row") * (height or rows) - top
    row = lax.broadcasted_iota(jnp.int32, (rows, slots2), 0) - r0
    row_pick = jnp.where((row >= 0) & (row < BOX_R), 1.0, 0.0)
    row_odd = row_pick * (2 * row - (BOX_R - 1)).astype(jnp.float32)

    def body(i, carry):
        w = weight[pl.ds(i * group, group)].reshape(group * rows, columns)
        high = w.astype(jnp.bfloat16)
        low = (w - high.astype(jnp.float32)).astype(jnp.bfloat16)
        table = sel[...]
        folded = jnp.dot(high, table, preferred_element_type=jnp.float32)
        folded = folded + jnp.dot(low, table, preferred_element_type=jnp.float32)
        for k in range(group):
            part = folded[k * rows : (k + 1) * rows]
            frame = first + i * group + k - f0
            pick = jnp.where((frame >= 0) & (frame < BOX_F), 1.0, 0.0)
            odd = pick * (2 * frame - (BOX_F - 1)).astype(jnp.float32)
            plain = jnp.sum(part * row_pick, axis=0, keepdims=True)
            by_row = jnp.sum(part * row_odd, axis=0, keepdims=True)
            carry = (carry[0] + plain * pick, carry[1] + plain * odd, carry[2] + by_row * pick)
        return carry

    return lax.fori_loop(0, count // group, body, start)


def halo_tile(z1, z2, index, j):
    sub, _ = iotas()
    even = row_is_even()
    shift1 = jnp.where(even, ZPAD, 0)
    head = (sub < SUB // 2) == even
    one = z1[j, pl.ds(2 * index + shift1, SUB), :]
    two = z2[j, pl.ds(2 * index + ZPAD - shift1, SUB), :]
    place = lax.axis_index("row")
    inside = (sub >= SUB // 2) | (place != lax.axis_size("row") - 1)
    inside = inside & ((sub < SUB // 2) | (place != 0))
    return jnp.where(inside, jnp.where(head, one, two), 0.0)


def edge_kernel(x, b0, sems):
    count, rows, _ = x.shape
    start = jnp.where(is_even(), 0, count - REACH)
    copies = [
        pltpu.make_async_copy(x.at[pl.ds(start, REACH), pl.ds(row, SUB)], b0.at[:, pl.ds(to, SUB)], sems.at[k])
        for k, (row, to) in enumerate(((0, 0), (rows - SUB, SUB)))
    ]
    for copy in copies:
        copy.start()
    for copy in copies:
        copy.wait()


def pack_kernel(x, near, rims, *rest):
    count, rows, _ = x.shape
    *pieces, sems = rest
    even = is_even()
    copies = [pltpu.make_async_copy(x.at[pl.ds(jnp.where(even, count - REACH, 0), REACH)], near, sems.at[0])]
    *targets, filtered1, filtered2, last = pieces
    for k, (begin, end) in enumerate(PIECES):
        start = jnp.where(even, begin, count - end)
        source = x.at[pl.ds(start, end - begin), pl.ds(SUB, rows - 2 * SUB)]
        copies.append(pltpu.make_async_copy(source, (*targets, last)[k], sems.at[k + 1]))
    for k, (row, to) in enumerate(((0, 0), (rows - SUB, SUB))):
        copies.append(
            pltpu.make_async_copy(x.at[:, pl.ds(row, SUB)], rims.at[:, pl.ds(to, SUB)], sems.at[len(PIECES) + 1 + k])
        )
    for copy in copies:
        copy.start()
    for copy in copies:
        copy.wait()
    _, lane = iotas()
    strips, part, _ = filtered1.shape
    for t in range(rows // SUB - 2):
        values = [last[0, rows_of(t), pl.ds(j * LANES, LANES)] for j in range(strips)]
        target, to = (filtered1, t) if t < part // SUB else (filtered2, t - part // SUB)
        for j, v in enumerate(column_sums(values, lane)):
            target[j, rows_of(to), :] = v


def rows_kernel(*refs):
    *sources, z1, z2 = refs
    _, _ = iotas()
    even = row_is_even()
    strips = z1.shape[0]
    for j in range(strips):
        at = pl.ds(j * LANES, LANES)
        k = ZPAD
        for z in (z1, z2):
            z[j, 0:SUB, :] = jnp.zeros((SUB, LANES), jnp.float32)
            z[j, pl.ds(z.shape[1] - SUB, SUB), :] = jnp.zeros((SUB, LANES), jnp.float32)
        for source in sources:
            rows = source.shape[1]
            for i in range(source.shape[0]):
                upper, lower = source[i, 0:2, at], source[i, rows - 2 : rows, at]
                z1[j, k : k + 2, :] = jnp.where(even, lower, upper)
                z2[j, k : k + 2, :] = jnp.where(even, upper, lower)
                k += 2


def table_kernel(boxes, sel):
    slots = boxes.shape[1] // 2
    step = lax.broadcasted_iota(jnp.int32, sel.shape, 0) - boxes[2:3, :]
    odd = lax.broadcasted_iota(jnp.int32, sel.shape, 1) >= slots
    value = jnp.where(odd, 2 * step - (BOX_C - 1), 1).astype(jnp.float32)
    inside = (step >= 0) & (step < BOX_C) & (boxes[0:1, :] >= 0)
    sel[...] = jnp.where(inside, value, 0.0).astype(jnp.bfloat16)


def early_kernel(
    x, a, z1, z2, level, sel, boxes, out, part, edge, sums, first, smooth, weight, sems, *, early
):
    count, rows, columns = x.shape
    tiles, strips = rows // SUB, columns // LANES
    even = is_even()

    def body(j, carry):
        at = pl.ds(pl.multiple_of(j * LANES, LANES), LANES)

        def load(p):
            if p >= count:
                return None
            if p < 0:
                index = jnp.where(even, -1 - p, REACH + p)
                return [a[index, rows_of(t), at] for t in range(tiles)] + [halo_tile(z1, z2, count + index, j)]
            index = jnp.where(even, count - 1 - p, p)
            return [x[index, rows_of(t), at] for t in range(tiles)] + [halo_tile(z1, z2, index, j)]

        window = load(-REACH)
        for p in range(1 - REACH, SPAN - REACH):
            window = [u + v for u, v in zip(window, load(p))]
        last_c = last_d = None
        for p in range(-2, count + 2):
            if p > -2:
                if p + BW < count:
                    window = [u + v for u, v in zip(window, load(p + BW))]
                window = [u - v for u, v in zip(window, load(p - BW - 1))]
            f = load(p)
            c = [-v for v in window] if f is None else [float(SPAN) * u - v for u, v in zip(f, window)]
            if last_c is not None:
                d = [u + v for u, v in zip(last_c, c)]
                if last_d is not None:
                    result = [u + v for u, v in zip(last_d, d)]
                    q = p - 1
                    if q <= early:
                        store_rows(first, q + 1, j, result)
                    else:
                        for t, v in enumerate(result):
                            part[q - early - 1, j, rows_of(t), :] = v
                last_d = d
            last_c = c
        return carry

    lax.fori_loop(0, strips, body, 0)
    smooth_stage(first, smooth, early + 2, 0, rows, strips)
    copy_edge = pltpu.make_async_copy(smooth.at[pl.ds(early, 2)], edge, sems.at[0])
    copy_edge.start()
    weigh(lambda i: (smooth, i), level, weight, lambda i: jnp.where(even, early - i, i - 1), early, rows, strips)
    start = jnp.where(even, count - early, 0)
    copy = pltpu.make_async_copy(weight, out.at[pl.ds(start, early)], sems.at[1])
    copy.start()
    zero = jnp.zeros((1, sel.shape[1]), jnp.float32)
    result = box_sums(weight, sel, boxes, start, count, (zero,) * 3)
    for i in range(3):
        sums[i : i + 1, :] = result[i]
    copy_edge.wait()
    copy.wait()


def late_kernel(part, b, b0, z1, z2, level, sel, boxes, sums, edge, *rest, count, piece):
    begin, end = piece
    late = end - begin
    ahead = end == REACH - 1
    if ahead:
        new_part, *rest = rest
    else:
        _, out, new_part, *rest = rest
    if ahead:
        new_edge, tail, weight, new_sums, first, smooth, sems = rest
        tails = (tail,)
    else:
        new_edge, new_sums, first, smooth, weight, sems = rest
        tails = ()
    rows, columns = level.shape[0], b0.shape[2]
    tiles, strips = rows // SUB, columns // LANES
    even = is_even()
    taps = frame_taps()
    early = count - REACH

    def body(j, carry):
        at = pl.ds(pl.multiple_of(j * LANES, LANES), LANES)

        def load_edges(q):
            where = jnp.where(even, REACH - 1 - q, q)
            return b0[where, rows_of(0), at], [b0[where, rows_of(1), at], halo_tile(z1, z2, where, j)]

        def load(q):
            index = jnp.where(even, end - 1 - q, q - begin)
            head, last = load_edges(q)
            return [head] + [b[index, rows_of(t), at] for t in range(tiles - 2)] + last

        def add(total, tap, values):
            if tap == -1.0:
                return [u - v for u, v in zip(total, values)]
            return [u + tap * v for u, v in zip(total, values)]

        fresh = {q: load(q) for q in range(begin, end)}
        for i in range(REACH - begin):
            total = [part[i, j, rows_of(t), :] for t in range(tiles + 1)]
            for q in range(begin, end):
                distance = REACH - 1 + q - begin - i
                if abs(distance) < REACH:
                    total = add(total, float(taps[abs(distance)]), fresh[q])
            if ahead and i == late:
                head, last = load_edges(end)
                tap = float(taps[REACH - 1])
                total = add(total[:1], tap, [head]) + total[1 : tiles - 1] + add(total[tiles - 1 :], tap, last)
            if i < late or ahead:
                store_rows(first, i, j, total)
            else:
                for t, v in enumerate(total):
                    new_part[i - late, j, rows_of(t), :] = v
        return carry

    lax.fori_loop(0, strips, body, 0)
    smooth_stage(first, smooth, late + 1 if ahead else late, 0, rows, strips)
    if ahead:
        copies = [
            pltpu.make_async_copy(smooth.at[late - 1], new_edge, sems.at[0]),
            pltpu.make_async_copy(smooth.at[late], new_part, sems.at[2]),
        ]
    else:
        copies = [pltpu.make_async_copy(smooth.at[pl.ds(late - 2, 2)], new_edge, sems.at[0])]
    for copy in copies:
        copy.start()
    weigh(
        lambda i: (edge, i) if i < 2 else (smooth, i - 2),
        level,
        weight,
        lambda i: jnp.where(even, late - i, i - 1),
        late,
        rows,
        strips,
        *tails,
    )
    place = jnp.where(even, REACH - end, early + begin)
    if not ahead:
        copies.append(pltpu.make_async_copy(weight, out.at[pl.ds(place, late)], sems.at[1]))
        copies[-1].start()
    start = tuple(sums[i : i + 1, :] for i in range(3))
    for i, v in enumerate(box_sums(weight, sel, boxes, place, count, start)):
        new_sums[i : i + 1, :] = v
    for copy in copies:
        copy.wait()


def last_kernel1(ready, fresh, level, sel, boxes, sums, centre, tail, weight, new_sums, padded, smooth, *, count):
    rows = level.shape[0]
    end = weight.shape[1] // SUB
    weigh_last(ready, (fresh,), padded, smooth, centre, tail, level, weight, rows, sel.shape[0] // LANES, 0, end)
    place = jnp.where(is_even(), 0, count - 1)
    start = tuple(sums[i : i + 1, :] for i in range(3))
    for i, v in enumerate(box_sums(weight, sel, boxes, place, count, start, 0, rows)):
        new_sums[i : i + 1, :] = v


def last_kernel2(
    ready, fresh1, fresh2, level, sel, boxes, sums, centre, tail, before, upper, _, out, stats, padded, smooth, weight,
    figures, sems
):
    count, rows, columns = out.shape
    done = upper.shape[1]
    even = is_even()
    place = jnp.where(even, 0, count - 1)
    copies = [
        pltpu.make_async_copy(before, out.at[pl.ds(jnp.where(even, 1, count - 2), 1)], sems.at[0]),
        pltpu.make_async_copy(upper, out.at[pl.ds(place, 1), pl.ds(0, done)], sems.at[1]),
        pltpu.make_async_copy(weight, out.at[pl.ds(place, 1), pl.ds(done, rows - done)], sems.at[2]),
        pltpu.make_async_copy(figures, stats, sems.at[3]),
    ]
    copies[0].start()
    copies[1].start()
    weigh_last(
        ready, (fresh1, fresh2), padded, smooth, centre, tail, level, weight, rows, columns // LANES, done // SUB,
        rows // SUB
    )
    copies[2].start()
    start = tuple(sums[i : i + 1, :] for i in range(3))
    total, by_frame, by_row = box_sums(weight, sel, boxes, place, count, start, done, rows)
    slots = stats.shape[1]
    cells = float(BOX_F * BOX_R * BOX_C)
    figures[0:1, :] = total[:, :slots] / cells
    figures[1:2, :] = by_frame[:, :slots] / (cells * (BOX_F - 1))
    figures[2:3, :] = by_row[:, :slots] / (cells * (BOX_R - 1))
    figures[3:4, :] = total[:, slots:] / (cells * (BOX_C - 1))
    copies[3].start()
    for copy in copies:
        copy.wait()


def shape(*sizes):
    return jax.ShapeDtypeStruct(sizes, jnp.float32)


def vmem():
    return pl.BlockSpec(memory_space=pltpu.VMEM)


def hbm():
    return pl.BlockSpec(memory_space=pltpu.HBM)


def row_exchange(sources, strips):
    ring, column = lax.axis_size("omega"), lax.axis_size("row")
    frames = sum(v.shape[0] for v in sources)
    rows = shape(strips, 2 * frames + 2 * ZPAD, LANES)
    z1, z2 = pl.pallas_call(
        rows_kernel,
        out_shape=(rows, rows),
        in_specs=[vmem()] * len(sources),
        out_specs=(vmem(), vmem()),
        compiler_params=pltpu.CompilerParams(vmem_limit_bytes=1 << 20),
    )(*sources)
    both = ("omega", "row")
    return (lax.ppermute(z1, both, row_pairs(ring, column, 0)), lax.ppermute(z2, both, row_pairs(ring, column, 1)))


def row_pairs(ring, column, start):
    pairs = []
    for i in range(ring):
        for r in range(column):
            mate = r + 1 if (r - start) % 2 == 0 else r - 1
            there = (i, mate) if 0 <= mate < column else (i ^ 1, r)
            pairs.append((i * column + r, there[0] * column + there[1]))
    return pairs


def steps(frames, thresholds, spot_boxes):
    count, rows, columns = frames.shape
    slots = spot_boxes.shape[1]
    early = count - REACH
    strips = columns // LANES
    cut = (rows // SUB - 2) * 2 // 3
    ring = lax.axis_size("omega")
    partner = [(i, i ^ 1) for i in range(ring)]
    other = [(i, (i - 1) % ring if i % 2 == 0 else (i + 1) % ring) for i in range(ring)]

    in_hbm = pltpu.with_memory_space_constraint(frames, pltpu.HBM)
    small = pltpu.CompilerParams(vmem_limit_bytes=1 << 20)
    edges = pl.pallas_call(
        edge_kernel,
        out_shape=shape(REACH, 2 * SUB, columns),
        in_specs=[hbm()],
        out_specs=vmem(),
        scratch_shapes=[pltpu.SemaphoreType.DMA((2,))],
        compiler_params=small,
        name="edge",
    )(in_hbm)
    b0 = lax.ppermute(edges, "omega", other)
    near, rims, *pieces = pl.pallas_call(
        pack_kernel,
        out_shape=(shape(REACH, rows, columns), shape(count, 2 * SUB, columns))
        + tuple(shape(end - begin, rows - 2 * SUB, columns) for begin, end in PIECES[:-1])
        + (shape(strips, cut * SUB, LANES), shape(strips, rows - (2 + cut) * SUB, LANES)),
        in_specs=[hbm()],
        out_specs=(vmem(),) * (3 + len(PIECES)),
        scratch_shapes=[
            pltpu.VMEM((1, rows - 2 * SUB, columns), jnp.float32),
            pltpu.SemaphoreType.DMA((3 + len(PIECES),)),
        ],
        compiler_params=small,
        name="pack",
    )(in_hbm)
    a = lax.ppermute(near, "omega", partner)
    pieces = [lax.ppermute(piece, "omega", other) for piece in pieces]
    z1, z2 = row_exchange([rims, a], strips)
    far1, far2 = row_exchange([b0], strips)

    level = jnp.broadcast_to((thresholds.astype(jnp.float32) / 64.0)[:, None], (rows, LANES))
    boxes = jnp.concatenate([spot_boxes, spot_boxes], axis=1)

    padded = rows + 2 * TOP
    sel = pl.pallas_call(
        table_kernel,
        out_shape=jax.ShapeDtypeStruct((columns, 2 * slots), jnp.bfloat16),
        in_specs=[vmem()],
        out_specs=vmem(),
        compiler_params=small,
        name="table",
    )(boxes)
    weight, part, edge, sums = pl.pallas_call(
        functools.partial(early_kernel, early=early),
        out_shape=(
            shape(count, rows, columns),
            shape(REACH, strips, rows + SUB, LANES),
            shape(2, strips, padded, LANES),
            shape(3, 2 * slots),
        ),
        in_specs=[vmem()] * 7,
        out_specs=(hbm(), vmem(), vmem(), vmem()),
        scratch_shapes=[
            pltpu.VMEM((early + 2, strips, padded, LANES), jnp.float32),
            pltpu.VMEM((early + 2, strips, padded, LANES), jnp.float32),
            pltpu.VMEM((early, rows, columns), jnp.float32),
            pltpu.SemaphoreType.DMA((2,)),
        ],
        compiler_params=pltpu.CompilerParams(vmem_limit_bytes=14 << 20),
        cost_estimate=pl.CostEstimate(flops=40 * frames.size, bytes_accessed=16 << 20, transcendentals=0),
        name="early",
    )(frames, a, z1, z2, level, sel, boxes)
    params = pltpu.CompilerParams(vmem_limit_bytes=14 << 20)
    strip = shape(strips, padded, LANES)
    for (begin, end), piece in zip(PIECES[:-1], pieces):
        late = end - begin
        ahead = end == REACH - 1
        made = late + 1 if ahead else late
        edges = shape(2, strips, padded, LANES)
        values = (part, piece, b0, far1, far2, level, sel, boxes, sums, edge)
        if ahead:
            handed = (strip, strip, shape(strips, rows, LANES), shape(late, rows, columns))
        else:
            handed = (shape(count, rows, columns), shape(REACH - end, strips, rows + SUB, LANES), edges)
            values = (*values, weight)
        scratch = [pltpu.VMEM((made, strips, padded, LANES), jnp.float32)] * 2
        if not ahead:
            scratch = scratch + [pltpu.VMEM((late, rows, columns), jnp.float32)]
        results = pl.pallas_call(
            functools.partial(late_kernel, count=count, piece=(begin, end)),
            out_shape=(*handed, shape(3, 2 * slots)),
            in_specs=[vmem()] * 10 + ([] if ahead else [hbm()]),
            out_specs=(vmem() if ahead else hbm(),) + (vmem(),) * len(handed),
            input_output_aliases={} if ahead else {10: 0},
            scratch_shapes=scratch + [pltpu.SemaphoreType.DMA((3,))],
            compiler_params=params,
            cost_estimate=pl.CostEstimate(flops=8 * late * rows * columns, bytes_accessed=4 << 20, transcendentals=0),
        )(*values)
        if ahead:
            part, edge, tail, before, sums = results
        else:
            weight, part, edge, sums = results
    done = cut * SUB
    upper, sums = pl.pallas_call(
        functools.partial(last_kernel1, count=count),
        out_shape=(shape(1, done, columns), shape(3, 2 * slots)),
        in_specs=[vmem()] * 8,
        out_specs=(vmem(), vmem()),
        scratch_shapes=[pltpu.VMEM((strips, padded, LANES), jnp.float32), pltpu.VMEM((1, strips, padded, LANES), jnp.float32)],
        compiler_params=params,
        cost_estimate=pl.CostEstimate(flops=4 * rows * columns, bytes_accessed=2 << 20, transcendentals=0),
        name="last1",
    )(part, pieces[-2], level, sel, boxes, sums, edge, tail)
    weight, stats = pl.pallas_call(
        last_kernel2,
        out_shape=(shape(count, rows, columns), shape(4, slots)),
        in_specs=[vmem()] * 11 + [hbm()],
        out_specs=(hbm(), hbm()),
        input_output_aliases={11: 0},
        scratch_shapes=[
            pltpu.VMEM((strips, padded, LANES), jnp.float32),
            pltpu.VMEM((1, strips, padded, LANES), jnp.float32),
            pltpu.VMEM((1, rows - done, columns), jnp.float32),
            pltpu.VMEM((4, slots), jnp.float32),
            pltpu.SemaphoreType.DMA((4,)),
        ],
        compiler_params=params,
        cost_estimate=pl.CostEstimate(flops=4 * rows * columns, bytes_accessed=2 << 20, transcendentals=0),
        name="last2",
    )(part, pieces[-2], pieces[-1], level, sel, boxes, sums, edge, tail, before, upper, weight)
    return weight, stats


def solution(mesh):
    return jax.shard_map(
        steps,
        mesh=mesh,
        in_specs=(P("omega", "row", None), P("row"), P(None, ("omega", "row"))),
        out_specs=(P("omega", "row", None), P(None, ("omega", "row"))),
        check_vma=False,
    )
```

```python
import functools

import jax
import jax.numpy as jnp
from jax import lax
from jax.experimental import pallas as pl
from jax.experimental.pallas import tpu as pltpu
from jax.sharding import PartitionSpec as P


BW = 4
BOX_F = 8
BOX_R = 16
BOX_C = 16
SHARP = 8.0

SUB = 8
LANES = 128
REACH = BW + 2
SPAN = 2 * BW + 1
NEG = -1e30
ZPAD = 6
TOP = 8
PIECES = ((0, 4), (4, 5), (5, 6))
SCALE = 1.0 / (SPAN * 64.0)


def frame_taps():
    three = {-1: 1, 0: 2, 1: 1}
    return [
        SPAN * three.get(d, 0) - sum(w for e, w in three.items() if abs(d - e) <= BW) for d in range(BW + 2)
    ]


def next_column(strips, lane, edge):
    rolled = [pltpu.roll(v, LANES - 1, 1) for v in strips] + [edge]
    return [jnp.where(lane == LANES - 1, rolled[j + 1], rolled[j]) for j in range(len(strips))]


def previous_column(strips, lane, edge):
    rolled = [edge] + [pltpu.roll(v, 1, 1) for v in strips]
    return [jnp.where(lane == 0, rolled[j], rolled[j + 1]) for j in range(len(strips))]


def column_sums(strips, lane):
    pairs = [a + b for a, b in zip(strips, next_column(strips, lane, jnp.zeros_like(strips[0])))]
    return [a + b for a, b in zip(pairs, previous_column(pairs, lane, strips[0]))]


def column_tops(strips, lane):
    tops = [jnp.maximum(a, b) for a, b in zip(strips, next_column(strips, lane, strips[-1]))]
    return [jnp.maximum(a, b) for a, b in zip(tops, previous_column(tops, lane, tops[0]))]


def iotas():
    sub = lax.broadcasted_iota(jnp.int32, (SUB, LANES), 0)
    lane = lax.broadcasted_iota(jnp.int32, (SUB, LANES), 1)
    return sub, lane


def is_even():
    return lax.rem(lax.axis_index("omega"), 2) == 0


def row_is_even():
    return lax.rem(lax.axis_index("row"), 2) == 0


def rows_of(t):
    return pl.ds(t * SUB, SUB)


def store_rows(ref, i, j, tiles):
    for t, v in enumerate(tiles[:-1]):
        ref[i, j, pl.ds(TOP + t * SUB, SUB), :] = v
    ref[i, j, pl.ds(0, SUB), :] = tiles[-1]
    ref[i, j, pl.ds(TOP + (len(tiles) - 1) * SUB, SUB), :] = tiles[-1]


def window_starts(rows):
    return [-1 + SUB * k for k in range(rows // SUB)] + [rows + 1 - SUB]


def smooth_window(first, i, smooth, o, start, rows, strips):
    sub, lane = iotas()
    place = lax.axis_index("row")
    seconds = []
    for j in range(strips):
        a, b, c = (first[i, j, pl.ds(TOP + start + e, SUB), :] for e in (-1, 0, 1))
        seconds.append((a + b) + (b + c))
    sums = column_sums(seconds, lane)
    for j in range(strips):
        v = sums[j]
        if start < 0:
            v = jnp.where((sub == 0) & (place == 0), NEG, v)
        if start + SUB > rows:
            v = jnp.where((sub == SUB - 1) & (place == lax.axis_size("row") - 1), NEG, v)
        smooth[o, j, pl.ds(TOP + start, SUB), :] = v


def smooth_stage(first, smooth, count, shift, rows, strips):
    def body(i, carry):
        for start in window_starts(rows):
            smooth_window(first, i, smooth, i + shift, start, rows, strips)
        return carry

    lax.fori_loop(0, count, body, 0)


def row_tops(ref, i, base, strips):
    loads = ([ref[i, j, pl.ds(base + e, SUB), :] for e in (-1, 0, 1)] for j in range(strips))
    return [jnp.maximum(jnp.maximum(a, b), c) for a, b, c in loads]


def weight_of(s, top, floor):
    return jnp.exp((SHARP * SCALE) * (s - top)) * jnp.maximum(s * SCALE - floor, 0.0)


def weigh(smooth_of, level, weight, place, count, rows, strips, tail=None):
    _, lane = iotas()

    def body(t, carry):
        base = t * SUB + TOP
        at = pl.ds(pl.multiple_of(t * SUB, SUB), SUB)
        tops_of = lambda i: row_tops(*smooth_of(i), base, strips)
        here = tops_of(1)
        before = [jnp.maximum(a, b) for a, b in zip(tops_of(0), here)]
        floor = level[at, :]
        for i in range(1, count + 1):
            after = tops_of(i + 1)
            pairs = [jnp.maximum(a, b) for a, b in zip(here, after)]
            highs = [jnp.maximum(a, b) for a, b in zip(before, pairs)]
            here, before = after, pairs
            tops = column_tops(highs, lane)
            ref, index = smooth_of(i)
            for j in range(strips):
                s = ref[index, j, pl.ds(base, SUB), :]
                weight[place(i), at, pl.ds(j * LANES, LANES)] = weight_of(s, tops[j], floor)
        if tail is not None:
            for j, v in enumerate(column_tops(before, lane)):
                tail[j, at, :] = v
        return carry

    lax.fori_loop(0, rows // SUB, body, 0)


def weigh_last(ready, freshes, padded, smooth, centre, tail, level, weight, rows, strips, first, end):
    _, lane = iotas()
    tap = float(frame_taps()[-1])
    starts = window_starts(rows)
    tiles = rows // SUB
    cut = freshes[0].shape[1] // SUB
    zero = jnp.zeros((SUB, LANES), jnp.float32)
    for j in range(strips):
        for t in range(max(first - 1, 0), min(end + 1, tiles)):
            if t == 0 or t == tiles - 1:
                v = zero
            elif t <= cut:
                v = freshes[0][j, rows_of(t - 1), :]
            else:
                v = freshes[1][j, rows_of(t - 1 - cut), :]
            padded[j, pl.ds(TOP + t * SUB, SUB), :] = v
    for k in range(first, end + 1):
        start = starts[k]
        for j in range(strips):
            v = ready[j, pl.ds(TOP + start, SUB), :]
            if 0 < k < len(starts) - 1:
                a, b, c = (padded[j, pl.ds(TOP + start + e, SUB), :] for e in (-1, 0, 1))
                v = v + tap * ((a + b) + (b + c))
            smooth[0, j, pl.ds(TOP + start, SUB), :] = v
        if k == first:
            continue
        t = k - 1
        base = t * SUB + TOP
        at = pl.ds(t * SUB, SUB)
        tops = column_tops(row_tops(smooth, 0, base, strips), lane)
        floor = level[at, :]
        for j in range(strips):
            s = centre[j, pl.ds(base, SUB), :]
            top = jnp.maximum(tops[j], tail[j, at, :])
            weight[0, rows_of(t - first), pl.ds(j * LANES, LANES)] = weight_of(s, top, floor)


def box_sums(weight, sel, boxes, first, frames, start, top=0, height=None):
    count, rows, columns = weight.shape
    group = 2 if count % 2 == 0 else 1
    slots2 = sel.shape[1]
    frame_base = lax.axis_index("omega") * frames
    live = boxes[0:1, :] >= 0
    f0 = jnp.where(live, boxes[0:1, :] - frame_base, -BOX_F - frames)
    r0 = boxes[1:2, :] - lax.axis_index("row") * (height or rows) - top
    row = lax.broadcasted_iota(jnp.int32, (rows, slots2), 0) - r0
    row_pick = jnp.where((row >= 0) & (row < BOX_R), 1.0, 0.0)
    row_odd = row_pick * (2 * row - (BOX_R - 1)).astype(jnp.float32)

    def body(i, carry):
        w = weight[pl.ds(i * group, group)].reshape(group * rows, columns)
        high = w.astype(jnp.bfloat16)
        low = (w - high.astype(jnp.float32)).astype(jnp.bfloat16)
        table = sel[...]
        both = jnp.concatenate([high, low], axis=0)
        folded = jnp.dot(both, table, preferred_element_type=jnp.float32)
        folded = folded[: group * rows] + folded[group * rows :]
        for k in range(group):
            part = folded[k * rows : (k + 1) * rows]
            frame = first + i * group + k - f0
            pick = jnp.where((frame >= 0) & (frame < BOX_F), 1.0, 0.0)
            odd = pick * (2 * frame - (BOX_F - 1)).astype(jnp.float32)
            plain = jnp.sum(part * row_pick, axis=0, keepdims=True)
            by_row = jnp.sum(part * row_odd, axis=0, keepdims=True)
            carry = (carry[0] + plain * pick, carry[1] + plain * odd, carry[2] + by_row * pick)
        return carry

    return lax.fori_loop(0, count // group, body, start)


def halo_tile(z1, z2, index, j):
    sub, _ = iotas()
    even = row_is_even()
    shift1 = jnp.where(even, ZPAD, 0)
    head = (sub < SUB // 2) == even
    one = z1[j, pl.ds(2 * index + shift1, SUB), :]
    two = z2[j, pl.ds(2 * index + ZPAD - shift1, SUB), :]
    place = lax.axis_index("row")
    inside = (sub >= SUB // 2) | (place != lax.axis_size("row") - 1)
    inside = inside & ((sub < SUB // 2) | (place != 0))
    return jnp.where(inside, jnp.where(head, one, two), 0.0)


def edge_kernel(x, b0, sems):
    count, rows, _ = x.shape
    start = jnp.where(is_even(), 0, count - REACH)
    copies = [
        pltpu.make_async_copy(x.at[start + i, pl.ds(row, SUB)], b0.at[i, pl.ds(to, SUB)], sems.at[2 * i + k])
        for i in range(REACH)
        for k, (row, to) in enumerate(((0, 0), (rows - SUB, SUB)))
    ]
    for copy in copies:
        copy.start()
    for copy in copies:
        copy.wait()


def pack_kernel(x, near, rims, *rest):
    count, rows, _ = x.shape
    *pieces, sems = rest
    even = is_even()
    copies = [pltpu.make_async_copy(x.at[pl.ds(jnp.where(even, count - REACH, 0), REACH)], near, sems.at[0])]
    *targets, filtered1, filtered2, last = pieces
    for k, (begin, end) in enumerate(PIECES):
        start = jnp.where(even, begin, count - end)
        source = x.at[pl.ds(start, end - begin), pl.ds(SUB, rows - 2 * SUB)]
        copies.append(pltpu.make_async_copy(source, (*targets, last)[k], sems.at[k + 1]))
    for k, (row, to) in enumerate(((0, 0), (rows - SUB, SUB))):
        copies.append(
            pltpu.make_async_copy(x.at[:, pl.ds(row, SUB)], rims.at[:, pl.ds(to, SUB)], sems.at[len(PIECES) + 1 + k])
        )
    for copy in copies:
        copy.start()
    for copy in copies:
        copy.wait()
    _, lane = iotas()
    strips, part, _ = filtered1.shape
    for t in range(rows // SUB - 2):
        values = [last[0, rows_of(t), pl.ds(j * LANES, LANES)] for j in range(strips)]
        target, to = (filtered1, t) if t < part // SUB else (filtered2, t - part // SUB)
        for j, v in enumerate(column_sums(values, lane)):
            target[j, rows_of(to), :] = v


def rows_kernel(*refs):
    *sources, z1, z2 = refs
    _, _ = iotas()
    even = row_is_even()
    strips = z1.shape[0]
    for j in range(strips):
        at = pl.ds(j * LANES, LANES)
        k = ZPAD
        for z in (z1, z2):
            z[j, 0:SUB, :] = jnp.zeros((SUB, LANES), jnp.float32)
            z[j, pl.ds(z.shape[1] - SUB, SUB), :] = jnp.zeros((SUB, LANES), jnp.float32)
        for source in sources:
            rows = source.shape[1]
            for i in range(source.shape[0]):
                upper, lower = source[i, 0:2, at], source[i, rows - 2 : rows, at]
                z1[j, k : k + 2, :] = jnp.where(even, lower, upper)
                z2[j, k : k + 2, :] = jnp.where(even, upper, lower)
                k += 2


def table_kernel(boxes, sel):
    slots = boxes.shape[1] // 2
    step = lax.broadcasted_iota(jnp.int32, sel.shape, 0) - boxes[2:3, :]
    odd = lax.broadcasted_iota(jnp.int32, sel.shape, 1) >= slots
    value = jnp.where(odd, 2 * step - (BOX_C - 1), 1).astype(jnp.float32)
    inside = (step >= 0) & (step < BOX_C) & (boxes[0:1, :] >= 0)
    sel[...] = jnp.where(inside, value, 0.0).astype(jnp.bfloat16)


def early_kernel(
    x, a, z1, z2, level, sel, boxes, out, part, edge, sums, first, smooth, weight, sems, *, early
):
    count, rows, columns = x.shape
    tiles, strips = rows // SUB, columns // LANES
    even = is_even()

    def body(j, carry):
        at = pl.ds(pl.multiple_of(j * LANES, LANES), LANES)

        def load(p):
            if p >= count:
                return None
            if p < 0:
                index = jnp.where(even, -1 - p, REACH + p)
                return [a[index, rows_of(t), at] for t in range(tiles)] + [halo_tile(z1, z2, count + index, j)]
            index = jnp.where(even, count - 1 - p, p)
            return [x[index, rows_of(t), at] for t in range(tiles)] + [halo_tile(z1, z2, index, j)]

        window = load(-REACH)
        for p in range(1 - REACH, SPAN - REACH):
            window = [u + v for u, v in zip(window, load(p))]
        last_c = last_d = None
        for p in range(-2, count + 2):
            if p > -2:
                if p + BW < count:
                    window = [u + v for u, v in zip(window, load(p + BW))]
                window = [u - v for u, v in zip(window, load(p - BW - 1))]
            f = load(p)
            c = [-v for v in window] if f is None else [float(SPAN) * u - v for u, v in zip(f, window)]
            if last_c is not None:
                d = [u + v for u, v in zip(last_c, c)]
                if last_d is not None:
                    result = [u + v for u, v in zip(last_d, d)]
                    q = p - 1
                    if q <= early:
                        store_rows(first, q + 1, j, result)
                    else:
                        for t, v in enumerate(result):
                            part[q - early - 1, j, rows_of(t), :] = v
                last_d = d
            last_c = c
        return carry

    lax.fori_loop(0, strips, body, 0)
    smooth_stage(first, smooth, early + 2, 0, rows, strips)
    copy_edge = pltpu.make_async_copy(smooth.at[pl.ds(early, 2)], edge, sems.at[0])
    copy_edge.start()
    weigh(lambda i: (smooth, i), level, weight, lambda i: jnp.where(even, early - i, i - 1), early, rows, strips)
    start = jnp.where(even, count - early, 0)
    copy = pltpu.make_async_copy(weight, out.at[pl.ds(start, early)], sems.at[1])
    copy.start()
    zero = jnp.zeros((1, sel.shape[1]), jnp.float32)
    result = box_sums(weight, sel, boxes, start, count, (zero,) * 3)
    for i in range(3):
        sums[i : i + 1, :] = result[i]
    copy_edge.wait()
    copy.wait()


def late_kernel(part, b, b0, z1, z2, level, sel, boxes, sums, edge, *rest, count, piece):
    begin, end = piece
    late = end - begin
    ahead = end == REACH - 1
    if ahead:
        new_part, *rest = rest
    else:
        _, out, new_part, *rest = rest
    if ahead:
        new_edge, tail, weight, new_sums, first, smooth, sems = rest
        tails = (tail,)
    else:
        new_edge, new_sums, first, smooth, weight, sems = rest
        tails = ()
    rows, columns = level.shape[0], b0.shape[2]
    tiles, strips = rows // SUB, columns // LANES
    even = is_even()
    taps = frame_taps()
    early = count - REACH

    def body(j, carry):
        at = pl.ds(pl.multiple_of(j * LANES, LANES), LANES)

        def load_edges(q):
            where = jnp.where(even, REACH - 1 - q, q)
            return b0[where, rows_of(0), at], [b0[where, rows_of(1), at], halo_tile(z1, z2, where, j)]

        def load(q):
            index = jnp.where(even, end - 1 - q, q - begin)
            head, last = load_edges(q)
            return [head] + [b[index, rows_of(t), at] for t in range(tiles - 2)] + last

        def add(total, tap, values):
            if tap == -1.0:
                return [u - v for u, v in zip(total, values)]
            return [u + tap * v for u, v in zip(total, values)]

        fresh = {q: load(q) for q in range(begin, end)}
        for i in range(REACH - begin):
            total = [part[i, j, rows_of(t), :] for t in range(tiles + 1)]
            for q in range(begin, end):
                distance = REACH - 1 + q - begin - i
                if abs(distance) < REACH:
                    total = add(total, float(taps[abs(distance)]), fresh[q])
            if ahead and i == late:
                head, last = load_edges(end)
                tap = float(taps[REACH - 1])
                total = add(total[:1], tap, [head]) + total[1 : tiles - 1] + add(total[tiles - 1 :], tap, last)
            if i < late or ahead:
                store_rows(first, i, j, total)
            else:
                for t, v in enumerate(total):
                    new_part[i - late, j, rows_of(t), :] = v
        return carry

    lax.fori_loop(0, strips, body, 0)
    smooth_stage(first, smooth, late + 1 if ahead else late, 0, rows, strips)
    if ahead:
        copies = [
            pltpu.make_async_copy(smooth.at[late - 1], new_edge, sems.at[0]),
            pltpu.make_async_copy(smooth.at[late], new_part, sems.at[2]),
        ]
    else:
        copies = [pltpu.make_async_copy(smooth.at[pl.ds(late - 2, 2)], new_edge, sems.at[0])]
    for copy in copies:
        copy.start()
    weigh(
        lambda i: (edge, i) if i < 2 else (smooth, i - 2),
        level,
        weight,
        lambda i: jnp.where(even, late - i, i - 1),
        late,
        rows,
        strips,
        *tails,
    )
    place = jnp.where(even, REACH - end, early + begin)
    if not ahead:
        copies.append(pltpu.make_async_copy(weight, out.at[pl.ds(place, late)], sems.at[1]))
        copies[-1].start()
    start = tuple(sums[i : i + 1, :] for i in range(3))
    for i, v in enumerate(box_sums(weight, sel, boxes, place, count, start)):
        new_sums[i : i + 1, :] = v
    for copy in copies:
        copy.wait()


def last_kernel1(ready, fresh, level, sel, boxes, sums, centre, tail, weight, new_sums, padded, smooth, *, count):
    rows = level.shape[0]
    end = weight.shape[1] // SUB
    weigh_last(ready, (fresh,), padded, smooth, centre, tail, level, weight, rows, sel.shape[0] // LANES, 0, end)
    place = jnp.where(is_even(), 0, count - 1)
    start = tuple(sums[i : i + 1, :] for i in range(3))
    for i, v in enumerate(box_sums(weight, sel, boxes, place, count, start, 0, rows)):
        new_sums[i : i + 1, :] = v


def last_kernel2(
    ready, fresh1, fresh2, level, sel, boxes, sums, centre, tail, before, upper, _, out, stats, padded, smooth, weight,
    figures, sems
):
    count, rows, columns = out.shape
    done = upper.shape[1]
    even = is_even()
    place = jnp.where(even, 0, count - 1)
    copies = [
        pltpu.make_async_copy(before, out.at[pl.ds(jnp.where(even, 1, count - 2), 1)], sems.at[0]),
        pltpu.make_async_copy(upper, out.at[pl.ds(place, 1), pl.ds(0, done)], sems.at[1]),
        pltpu.make_async_copy(weight, out.at[pl.ds(place, 1), pl.ds(done, rows - done)], sems.at[2]),
        pltpu.make_async_copy(figures, stats, sems.at[3]),
    ]
    copies[0].start()
    copies[1].start()
    weigh_last(
        ready, (fresh1, fresh2), padded, smooth, centre, tail, level, weight, rows, columns // LANES, done // SUB,
        rows // SUB
    )
    copies[2].start()
    start = tuple(sums[i : i + 1, :] for i in range(3))
    total, by_frame, by_row = box_sums(weight, sel, boxes, place, count, start, done, rows)
    slots = stats.shape[1]
    cells = float(BOX_F * BOX_R * BOX_C)
    figures[0:1, :] = total[:, :slots] / cells
    figures[1:2, :] = by_frame[:, :slots] / (cells * (BOX_F - 1))
    figures[2:3, :] = by_row[:, :slots] / (cells * (BOX_R - 1))
    figures[3:4, :] = total[:, slots:] / (cells * (BOX_C - 1))
    copies[3].start()
    for copy in copies:
        copy.wait()


def shape(*sizes):
    return jax.ShapeDtypeStruct(sizes, jnp.float32)


def vmem():
    return pl.BlockSpec(memory_space=pltpu.VMEM)


def hbm():
    return pl.BlockSpec(memory_space=pltpu.HBM)


def row_exchange(sources, strips):
    ring, column = lax.axis_size("omega"), lax.axis_size("row")
    frames = sum(v.shape[0] for v in sources)
    rows = shape(strips, 2 * frames + 2 * ZPAD, LANES)
    z1, z2 = pl.pallas_call(
        rows_kernel,
        out_shape=(rows, rows),
        in_specs=[vmem()] * len(sources),
        out_specs=(vmem(), vmem()),
        compiler_params=pltpu.CompilerParams(vmem_limit_bytes=1 << 20),
    )(*sources)
    both = ("omega", "row")
    return (lax.ppermute(z1, both, row_pairs(ring, column, 0)), lax.ppermute(z2, both, row_pairs(ring, column, 1)))


def row_pairs(ring, column, start):
    pairs = []
    for i in range(ring):
        for r in range(column):
            mate = r + 1 if (r - start) % 2 == 0 else r - 1
            there = (i, mate) if 0 <= mate < column else (i ^ 1, r)
            pairs.append((i * column + r, there[0] * column + there[1]))
    return pairs


def steps(frames, thresholds, spot_boxes):
    count, rows, columns = frames.shape
    slots = spot_boxes.shape[1]
    early = count - REACH
    strips = columns // LANES
    cut = rows // SUB - 3
    ring = lax.axis_size("omega")
    partner = [(i, i ^ 1) for i in range(ring)]
    other = [(i, (i - 1) % ring if i % 2 == 0 else (i + 1) % ring) for i in range(ring)]

    in_hbm = pltpu.with_memory_space_constraint(frames, pltpu.HBM)
    small = pltpu.CompilerParams(vmem_limit_bytes=1 << 20)
    edges = pl.pallas_call(
        edge_kernel,
        out_shape=shape(REACH, 2 * SUB, columns),
        in_specs=[hbm()],
        out_specs=vmem(),
        scratch_shapes=[pltpu.SemaphoreType.DMA((2 * REACH,))],
        compiler_params=small,
        name="edge",
    )(in_hbm)
    b0 = lax.ppermute(edges, "omega", other)
    near, rims, *pieces = pl.pallas_call(
        pack_kernel,
        out_shape=(shape(REACH, rows, columns), shape(count, 2 * SUB, columns))
        + tuple(shape(end - begin, rows - 2 * SUB, columns) for begin, end in PIECES[:-1])
        + (shape(strips, cut * SUB, LANES), shape(strips, rows - (2 + cut) * SUB, LANES)),
        in_specs=[hbm()],
        out_specs=(vmem(),) * (3 + len(PIECES)),
        scratch_shapes=[
            pltpu.VMEM((1, rows - 2 * SUB, columns), jnp.float32),
            pltpu.SemaphoreType.DMA((3 + len(PIECES),)),
        ],
        compiler_params=small,
        name="pack",
    )(in_hbm)
    a = lax.ppermute(near, "omega", partner)
    pieces = [lax.ppermute(piece, "omega", other) for piece in pieces]
    z1, z2 = row_exchange([rims, a], strips)
    far1, far2 = row_exchange([b0], strips)

    level = jnp.broadcast_to((thresholds.astype(jnp.float32) / 64.0)[:, None], (rows, LANES))
    boxes = jnp.concatenate([spot_boxes, spot_boxes], axis=1)

    padded = rows + 2 * TOP
    sel = pl.pallas_call(
        table_kernel,
        out_shape=jax.ShapeDtypeStruct((columns, 2 * slots), jnp.bfloat16),
        in_specs=[vmem()],
        out_specs=vmem(),
        compiler_params=small,
        name="table",
    )(boxes)
    weight, part, edge, sums = pl.pallas_call(
        functools.partial(early_kernel, early=early),
        out_shape=(
            shape(count, rows, columns),
            shape(REACH, strips, rows + SUB, LANES),
            shape(2, strips, padded, LANES),
            shape(3, 2 * slots),
        ),
        in_specs=[vmem()] * 7,
        out_specs=(hbm(), vmem(), vmem(), vmem()),
        scratch_shapes=[
            pltpu.VMEM((early + 2, strips, padded, LANES), jnp.float32),
            pltpu.VMEM((early + 2, strips, padded, LANES), jnp.float32),
            pltpu.VMEM((early, rows, columns), jnp.float32),
            pltpu.SemaphoreType.DMA((2,)),
        ],
        compiler_params=pltpu.CompilerParams(vmem_limit_bytes=14 << 20),
        cost_estimate=pl.CostEstimate(flops=40 * frames.size, bytes_accessed=16 << 20, transcendentals=0),
        name="early",
    )(frames, a, z1, z2, level, sel, boxes)
    params = pltpu.CompilerParams(vmem_limit_bytes=14 << 20)
    strip = shape(strips, padded, LANES)
    for (begin, end), piece in zip(PIECES[:-1], pieces):
        late = end - begin
        ahead = end == REACH - 1
        made = late + 1 if ahead else late
        edges = shape(2, strips, padded, LANES)
        values = (part, piece, b0, far1, far2, level, sel, boxes, sums, edge)
        if ahead:
            handed = (strip, strip, shape(strips, rows, LANES), shape(late, rows, columns))
        else:
            handed = (shape(count, rows, columns), shape(REACH - end, strips, rows + SUB, LANES), edges)
            values = (*values, weight)
        scratch = [pltpu.VMEM((made, strips, padded, LANES), jnp.float32)] * 2
        if not ahead:
            scratch = scratch + [pltpu.VMEM((late, rows, columns), jnp.float32)]
        results = pl.pallas_call(
            functools.partial(late_kernel, count=count, piece=(begin, end)),
            out_shape=(*handed, shape(3, 2 * slots)),
            in_specs=[vmem()] * 10 + ([] if ahead else [hbm()]),
            out_specs=(vmem() if ahead else hbm(),) + (vmem(),) * len(handed),
            input_output_aliases={} if ahead else {10: 0},
            scratch_shapes=scratch + [pltpu.SemaphoreType.DMA((3,))],
            compiler_params=params,
            cost_estimate=pl.CostEstimate(flops=8 * late * rows * columns, bytes_accessed=4 << 20, transcendentals=0),
        )(*values)
        if ahead:
            part, edge, tail, before, sums = results
        else:
            weight, part, edge, sums = results
    done = cut * SUB
    upper, sums = pl.pallas_call(
        functools.partial(last_kernel1, count=count),
        out_shape=(shape(1, done, columns), shape(3, 2 * slots)),
        in_specs=[vmem()] * 8,
        out_specs=(vmem(), vmem()),
        scratch_shapes=[pltpu.VMEM((strips, padded, LANES), jnp.float32), pltpu.VMEM((1, strips, padded, LANES), jnp.float32)],
        compiler_params=params,
        cost_estimate=pl.CostEstimate(flops=4 * rows * columns, bytes_accessed=2 << 20, transcendentals=0),
        name="last1",
    )(part, pieces[-2], level, sel, boxes, sums, edge, tail)
    weight, stats = pl.pallas_call(
        last_kernel2,
        out_shape=(shape(count, rows, columns), shape(4, slots)),
        in_specs=[vmem()] * 11 + [hbm()],
        out_specs=(hbm(), hbm()),
        input_output_aliases={11: 0},
        scratch_shapes=[
            pltpu.VMEM((strips, padded, LANES), jnp.float32),
            pltpu.VMEM((1, strips, padded, LANES), jnp.float32),
            pltpu.VMEM((1, rows - done, columns), jnp.float32),
            pltpu.VMEM((4, slots), jnp.float32),
            pltpu.SemaphoreType.DMA((4,)),
        ],
        compiler_params=params,
        cost_estimate=pl.CostEstimate(flops=4 * rows * columns, bytes_accessed=2 << 20, transcendentals=0),
        name="last2",
    )(part, pieces[-2], pieces[-1], level, sel, boxes, sums, edge, tail, before, upper, weight)
    return weight, stats


def solution(mesh):
    return jax.shard_map(
        steps,
        mesh=mesh,
        in_specs=(P("omega", "row", None), P("row"), P(None, ("omega", "row"))),
        out_specs=(P("omega", "row", None), P(None, ("omega", "row"))),
        check_vma=False,
    )
```
